32 devices in a mesh: dp: 4 (over z), seq: 2 (over y), mp: 4 (over x, core).
Axes of the slice: x: 2, y: 2, z: 4, core: 2. Of those that a mesh axis runs over, the one named last changes fastest.
Arguments:
- tokens: bfloat16 [2, 4, 1024, 2048], P(None, 'dp', 'seq'), may hold values from -6 to 6
- prefix: int32 [2, 4], P(None, 'dp'), may hold values from 102 to 512
- cotangent: bfloat16 [2, 4, 1024, 2048], P(None, 'dp', 'seq'), may hold values from -6 to 6
- ln1_gain: bfloat16 [2048], P(('dp', 'seq')), may hold values from 0.25 to 1.75
- ln1_bias: bfloat16 [2048], P(('dp', 'seq')), may hold values from -3 to 3
- qkv_weight: bfloat16 [2048, 3, 32, 64], P(('dp', 'seq'), None, 'mp'), may hold values from -0.125 to 0.125
- qv_bias: bfloat16 [2, 32, 64], P(None, 'mp', ('dp', 'seq')), may hold values from -3 to 3
- out_weight: bfloat16 [32, 64, 2048], P('mp', None, ('dp', 'seq')), may hold values from -0.25 to 0.25
- out_bias: bfloat16 [2048], P(('dp', 'seq')), may hold values from -3 to 3
- ln2_gain: bfloat16 [2048], P(('dp', 'seq')), may hold values from 0.25 to 1.75
- ln2_bias: bfloat16 [2048], P(('dp', 'seq')), may hold values from -3 to 3
- up_weight: bfloat16 [2048, 8192], P(('dp', 'seq'), 'mp'), may hold values from -0.125 to 0.125
- up_bias: bfloat16 [128, 64], P('mp', ('dp', 'seq')), may hold values from -3 to 3
- down_weight: bfloat16 [8192, 2048], P('mp', ('dp', 'seq')), may hold values from -0.0625 to 0.0625
- down_bias: bfloat16 [2048], P(('dp', 'seq')), may hold values from -3 to 3
Outputs:
- output: bfloat16 [2, 4, 1024, 2048], P(None, 'dp', 'seq')
- input_grad: bfloat16 [2, 4, 1024, 2048], P(None, 'dp', 'seq')
- ln1_gain_grad: float32 [2048], P(('dp', 'seq'))
- ln1_bias_grad: float32 [2048], P(('dp', 'seq'))
- qkv_weight_grad: float32 [2048, 3, 32, 64], P(('dp', 'seq'), None, 'mp')
- qv_bias_grad: float32 [2, 32, 64], P(None, 'mp', ('dp', 'seq'))
- out_weight_grad: float32 [32, 64, 2048], P('mp', None, ('dp', 'seq'))
- out_bias_grad: float32 [2048], P(('dp', 'seq'))
- ln2_gain_grad: float32 [2048], P(('dp', 'seq'))
- ln2_bias_grad: float32 [2048], P(('dp', 'seq'))
- up_weight_grad: float32 [2048, 8192], P(('dp', 'seq'), 'mp')
- up_bias_grad: float32 [128, 64], P('mp', ('dp', 'seq'))
- down_weight_grad: float32 [8192, 2048], P('mp', ('dp', 'seq'))
- down_bias_grad: float32 [2048], P(('dp', 'seq'))
The draws below stay inside these ranges and needn't reach their ends.
All inputs are finite; a program needn't handle non-finite values.
Results may differ from the reference program's by a relative error of at most 0.02.
Values may be sent and summed in bfloat16 or wider, within the bound.
No kernel may reach another device: no remote copies, remote signals or barrier semaphores. Data moves between devices by JAX's collectives and lax.ppermute only.
A program may use at most 256 MiB of HBM per device.

```python
import jax
import jax.numpy as jnp
from jax import lax

D = 2048
H = 32
FF = 8192
HD = 64
MICRO = 2
BATCH = 4
LENGTH = 1024


def touch_ends(entries, stream_key, least, largest):
    dims = entries.shape
    place = [jax.random.randint(jax.random.fold_in(stream_key, axis), (), 0, dims[axis]) for axis in range(len(dims))]
    entries = entries.at[tuple(place)].set(least)
    longest = dims.index(max(dims))
    place[longest] = (place[longest] + 1) % dims[longest]
    return entries.at[tuple(place)].set(largest)


def block_scale(own_key, extent, pieces, least, high):
    def one(dim, parts):
        draws = jax.random.uniform(jax.random.fold_in(jax.random.fold_in(own_key, 6), dim), (parts,), jnp.float32, least / len(pieces), high / len(pieces))
        return jnp.repeat(jnp.exp(draws), extent[dim] // parts).reshape((-1,) + (1,) * (len(extent) - dim - 1))

    factor_of = one(*pieces[0])
    for cut in pieces[1:]:
        factor_of = factor_of * one(*cut)
    return factor_of


def bell_draw(own_key, extent, scale, bound, cuts=(), kind=jnp.bfloat16):
    loudness = block_scale(own_key, extent, cuts, -0.22, 0.18) if cuts else 1.0
    values = jax.random.normal(own_key, extent, jnp.float32) * scale * loudness
    return jnp.minimum(jnp.maximum(values, -bound), bound).astype(kind)


def setup_inputs(seed: int = 0) -> dict:
    arg_keys = jax.random.split(jax.random.key(seed), 16)
    return {
        "tokens": bell_draw(arg_keys[0], (MICRO, BATCH, LENGTH, D), 1.0, 6.0, ((1, 4), (2, 2))),
        "prefix": touch_ends(jax.random.randint(arg_keys[1], (MICRO, BATCH), LENGTH // 10, LENGTH // 2 + 1), jax.random.fold_in(arg_keys[1], 1), LENGTH // 10, (LENGTH // 2 + 1) - 1).astype(jnp.int32),
        "cotangent": bell_draw(arg_keys[2], (MICRO, BATCH, LENGTH, D), 1.0, 6.0, ((1, 4), (2, 2))),
        "ln1_gain": jnp.clip(1.0 + 0.15 * jax.random.normal(arg_keys[3], (D,), jnp.float32), 0.25, 1.75).astype(jnp.bfloat16),
        "ln1_bias": bell_draw(arg_keys[4], (D,), 0.2, 3.0, ((0, 8),)),
        "qkv_weight": bell_draw(arg_keys[5], (D, 3, H, HD), D ** -0.5, 0.125, ((0, 8), (2, 4))),
        "qv_bias": bell_draw(arg_keys[6], (2, H, HD), 0.3, 3.0, ((1, 4), (2, 8))),
        "out_weight": bell_draw(arg_keys[7], (H, HD, D), (D // 4) ** -0.5, 0.25, ((0, 4), (2, 8))),
        "out_bias": bell_draw(arg_keys[8], (D,), 0.2, 3.0, ((0, 8),)),
        "ln2_gain": jnp.clip(1.0 + 0.15 * jax.random.normal(arg_keys[9], (D,), jnp.float32), 0.25, 1.75).astype(jnp.bfloat16),
        "ln2_bias": bell_draw(arg_keys[10], (D,), 0.2, 3.0, ((0, 8),)),
        "up_weight": bell_draw(arg_keys[11], (D, FF), D ** -0.5, 0.125, ((0, 8), (1, 4))),
        "up_bias": bell_draw(arg_keys[12], (FF // 64, 64), 0.3, 3.0, ((0, 4), (1, 8))),
        "down_weight": bell_draw(arg_keys[13], (FF, D), FF ** -0.5, 0.0625, ((0, 4), (1, 8))),
        "down_bias": bell_draw(arg_keys[14], (D,), 0.2, 3.0, ((0, 8),)),
    }


@jax.custom_vjp
def low(v):
    return lax.optimization_barrier(v.astype(jnp.bfloat16)).astype(jnp.float32)

@jax.custom_vjp
def low_back(v):
    return v

def low_keep(v):
    return (low(v), None)

def low_pass(kept, grad):
    return (grad,)

def back_keep(v):
    return (v, None)

def back_low(kept, grad):
    return (low(grad),)
low.defvjp(low_keep, low_pass)
low_back.defvjp(back_keep, back_low)
highest = lax.Precision.HIGHEST
eps_norm = 1e-05
masked_score = -1e+30

def normalize(values, gain_vec, shift_vec):
    row_mean = lax.optimization_barrier(jnp.mean(values, axis=-1, keepdims=True))
    centered = values - row_mean
    variance = lax.optimization_barrier(jnp.mean(centered * centered, axis=-1, keepdims=True))
    return centered * lax.rsqrt(variance + eps_norm) * gain_vec + shift_vec

def head_attention(queries, key_heads, value_heads, slope_h, distance, visible, score_scale):
    raw_scores = jnp.dot(queries, key_heads.T, precision=highest) * score_scale - slope_h * distance
    scores = jnp.where(visible, low_back(raw_scores), masked_score)
    row_max = lax.optimization_barrier(jnp.max(scores, axis=-1, keepdims=True))
    exp_scores = jnp.exp(scores - row_max)
    attn_probs = exp_scores / lax.optimization_barrier(jnp.sum(exp_scores, axis=-1, keepdims=True))
    return jnp.dot(low(attn_probs), value_heads, precision=highest)

def sequence_forward(params, seq_tokens, seq_prefix):
    gain_one, bias_one, w_qkv, bias_qv, w_out, bias_out, gain_two, bias_two, w_up, bias_up, w_down, bias_down = params
    h_one = low(normalize(seq_tokens, gain_one, bias_one))
    qkv_shift = jnp.concatenate([bias_qv[0].reshape(D), jnp.zeros((D,), jnp.float32), bias_qv[1].reshape(D)])
    qkv_all = jnp.dot(h_one, w_qkv.reshape(D, 3 * D), precision=highest) + qkv_shift
    qkv_all = low_back(low(qkv_all))
    head_parts = qkv_all.reshape(LENGTH, 3, H, HD).transpose(1, 2, 0, 3)
    positions = jnp.arange(LENGTH, dtype=jnp.int32)
    distance = jnp.abs(positions[:, None] - positions[None, :]).astype(jnp.float32)
    visible = (positions[None, :] <= positions[:, None]) | (positions[None, :] < seq_prefix)
    slopes = jnp.exp2(-8.0 * (jnp.arange(H, dtype=jnp.int32) + 1).astype(jnp.float32) / H)
    score_scale = HD ** (-0.5)

    def one_head(head_item):
        return head_attention(head_item[0], head_item[1], head_item[2], head_item[3], distance, visible, score_scale)
    head_outs = lax.map(jax.checkpoint(one_head), (head_parts[0], head_parts[1], head_parts[2], slopes))
    attn_flat = low_back(low(head_outs.transpose(1, 0, 2).reshape(LENGTH, D)))
    branch = low_back(jnp.dot(attn_flat, w_out.reshape(D, D), precision=highest) + bias_out)
    resid = seq_tokens + branch
    h_two = low(normalize(resid, gain_two, bias_two))
    up_pre = low_back(jnp.dot(h_two, w_up, precision=highest) + bias_up.reshape(FF))
    act_low = low(jax.nn.gelu(up_pre, approximate=False))
    return resid + jnp.dot(act_low, w_down, precision=highest) + bias_down

def reference(tokens, prefix, cotangent, ln1_gain, ln1_bias, qkv_weight, qv_bias, out_weight, out_bias, ln2_gain, ln2_bias, up_weight, up_bias, down_weight, down_bias):
    params = tuple((weight_arr.astype(jnp.float32) for weight_arr in (ln1_gain, ln1_bias, qkv_weight, qv_bias, out_weight, out_bias, ln2_gain, ln2_bias, up_weight, up_bias, down_weight, down_bias)))
    flat_tokens = tokens.reshape(MICRO * BATCH, LENGTH, D).astype(jnp.float32)
    flat_cot = cotangent.reshape(MICRO * BATCH, LENGTH, D).astype(jnp.float32)
    flat_prefix = prefix.reshape(MICRO * BATCH)

    def one_sequence(totals, seq_item):
        seq_tokens, seq_cot, seq_prefix = seq_item
        seq_out, pullback = jax.vjp(lambda param_set, token_set: sequence_forward(param_set, token_set, seq_prefix), params, seq_tokens)
        param_grads, token_grad = pullback(seq_cot)
        totals = jax.tree.map(lambda left, right: left + right, totals, param_grads)
        return (totals, (seq_out.astype(jnp.bfloat16), token_grad.astype(jnp.bfloat16)))
    zero_grads = jax.tree.map(jnp.zeros_like, params)
    totals, (seq_outs, token_grads) = lax.scan(one_sequence, zero_grads, (flat_tokens, flat_cot, flat_prefix))
    output = seq_outs.reshape(MICRO, BATCH, LENGTH, D)
    input_grad = token_grads.reshape(MICRO, BATCH, LENGTH, D)
    return (output, input_grad, totals[0], totals[1], totals[2], totals[3], totals[4], totals[5], totals[6], totals[7], totals[8], totals[9], totals[10], totals[11])
```

```python
import functools
import math

import jax
import jax.numpy as jnp
from jax import lax
from jax.experimental import pallas as pl
from jax.experimental.pallas import tpu as pltpu
from jax.sharding import PartitionSpec as P

eps_norm = 1e-05
masked_score = -1e30
inv_root_two = 0.7071067811865476
inv_root_tau = 0.3989422804014327


def contract_rows(left, right):
    return lax.dot_general(
        left, right, (((0,), (0,)), ((), ())), preferred_element_type=jnp.float32
    )


def contract_cols(left, right):
    return lax.dot_general(
        left, right, (((1,), (1,)), ((), ())), preferred_element_type=jnp.float32
    )


def normalize(values, gain_vec, shift_vec):
    row_mean = jnp.mean(values, axis=-1, keepdims=True)
    centered = values - row_mean
    variance = jnp.mean(centered * centered, axis=-1, keepdims=True)
    scale_inv = lax.rsqrt(variance + eps_norm)
    normed = centered * scale_inv
    return (normed * gain_vec + shift_vec, normed, scale_inv)


def normalize_back(grad_in, normed, scale_inv, gain_vec):
    scaled = grad_in * gain_vec
    return scale_inv * (
        scaled
        - jnp.mean(scaled, axis=-1, keepdims=True)
        - normed * jnp.mean(scaled * normed, axis=-1, keepdims=True)
    )


def gelu_slope(pre_act):
    cumulative = 0.5 * (1.0 + lax.erf(pre_act * inv_root_two))
    return cumulative + pre_act * jnp.exp(-0.5 * pre_act * pre_act) * inv_root_tau


def head_scores(queries, key_heads, slope_h, distance, visible, score_scale):
    raw_scores = contract_cols(queries, key_heads) * score_scale - slope_h * distance
    return jnp.where(visible, raw_scores, masked_score)


def split_heads(flat, count):
    return flat.reshape(flat.shape[0], count, -1).transpose(1, 0, 2)


def join_heads(stacked):
    return stacked.transpose(1, 0, 2).reshape(stacked.shape[1], -1)


log2e = math.log2(math.e)
hidden_distance = 1e30


def dot_nn(left, right):
    return lax.dot_general(
        left, right, (((1,), (0,)), ((), ())), preferred_element_type=jnp.float32
    )


def dot_nt(left, right):
    return lax.dot_general(
        left, right, (((1,), (1,)), ((), ())), preferred_element_type=jnp.float32
    )


def fill_distance(place_ref, dist_ref, rows):
    own_first, other_first = place_ref[0], place_ref[1]
    prefix, flip = place_ref[2], place_ref[3]
    for block, first in enumerate((own_first, other_first)):
        shape = (rows, rows)
        key_pos = (lax.broadcasted_iota(jnp.int32, shape, 0) ^ flip) + first
        query_pos = (lax.broadcasted_iota(jnp.int32, shape, 1) ^ flip) + own_first
        visible = (key_pos <= query_pos) | (key_pos < prefix)
        gap = jnp.abs(query_pos - key_pos).astype(jnp.float32)
        dist_ref[block * rows : (block + 1) * rows, :] = jnp.where(visible, gap, hidden_distance)


def attend_kernel(place_ref, slope_ref, q_ref, k_ref, v_ref, ko_ref, vo_ref, out_ref, lse_ref, dist_ref, *, head_size):
    pair = pl.program_id(0)
    rows = q_ref.shape[0]

    @pl.when(pair == 0)
    def _():
        fill_distance(place_ref, dist_ref, rows)

    per_block = q_ref.shape[1] // head_size
    queries = q_ref[...]
    keys = jnp.concatenate([k_ref[...], ko_ref[...]], axis=0)
    values_t = jnp.concatenate([v_ref[...], vo_ref[...]], axis=0).T
    lane_head = lax.broadcasted_iota(jnp.int32, queries.shape, 1) // head_size
    parts = []
    for head in range(per_block):
        picked = jnp.where(lane_head == head, queries, jnp.zeros_like(queries))
        slope = slope_ref[pair * per_block + head]
        scores = dot_nt(keys, picked) * (log2e * head_size**-0.5) - dist_ref[...] * slope
        top = jnp.max(scores, axis=0, keepdims=True)
        weights = jnp.exp2(scores - top)
        total = jnp.sum(weights, axis=0, keepdims=True)
        head_out = dot_nn(values_t, weights.astype(jnp.bfloat16)) / total
        parts.append(head_out[head * head_size : (head + 1) * head_size])
        lse_ref[pl.ds(pair * per_block + head, 1), :] = top + jnp.log2(total)
    out_ref[...] = jnp.concatenate(parts, axis=0).T.astype(out_ref.dtype)


def attend_back_kernel(
    place_ref, slope_ref, q_ref, k_ref, v_ref, ko_ref, vo_ref, g_ref, lse_ref,
    dq_ref, dk_ref, dv_ref, dko_ref, dvo_ref, dist_ref, *, head_size
):
    pair = pl.program_id(0)
    rows = q_ref.shape[0]

    @pl.when(pair == 0)
    def _():
        fill_distance(place_ref, dist_ref, rows)

    per_block = q_ref.shape[1] // head_size
    queries, grads = q_ref[...], g_ref[...]
    keys = jnp.concatenate([k_ref[...], ko_ref[...]], axis=0)
    values = jnp.concatenate([v_ref[...], vo_ref[...]], axis=0)
    keys_t = keys.T
    lane_head = lax.broadcasted_iota(jnp.int32, queries.shape, 1) // head_size
    dq_parts = []
    d_keys, d_values = None, None
    for head in range(per_block):
        here = lane_head == head
        picked = jnp.where(here, queries, jnp.zeros_like(queries))
        picked_grad = jnp.where(here, grads, jnp.zeros_like(grads))
        slope = slope_ref[pair * per_block + head]
        scores = dot_nt(keys, picked) * (log2e * head_size**-0.5) - dist_ref[...] * slope
        probs = jnp.exp2(scores - lse_ref[pl.ds(pair * per_block + head, 1), :])
        weighted = dot_nt(values, picked_grad) * probs
        delta = jnp.sum(weighted, axis=0, keepdims=True)
        d_scores = (weighted - probs * delta).astype(jnp.bfloat16)
        value_part = dot_nn(probs.astype(jnp.bfloat16), picked_grad)
        key_part = dot_nn(d_scores, picked)
        d_values = value_part if d_values is None else d_values + value_part
        d_keys = key_part if d_keys is None else d_keys + key_part
        dq_part = dot_nn(keys_t, d_scores)
        dq_parts.append(dq_part[head * head_size : (head + 1) * head_size])
    scale = head_size**-0.5
    dq_ref[...] = (jnp.concatenate(dq_parts, axis=0).T * scale).astype(dq_ref.dtype)
    dk_ref[...] = (d_keys[:rows] * scale).astype(dk_ref.dtype)
    dko_ref[...] = (d_keys[rows:] * scale).astype(dko_ref.dtype)
    dv_ref[...] = d_values[:rows].astype(dv_ref.dtype)
    dvo_ref[...] = d_values[rows:].astype(dvo_ref.dtype)


def column_block(rows, width, first):
    return pl.BlockSpec((rows, width), lambda step: (0, first + step))


def attend(qkv_rows, other_kv, place, slopes, head_size):
    rows, width = qkv_rows.shape[0], qkv_rows.shape[1] // 3
    wide = 2 * head_size
    steps = width // wide
    heads = width // head_size
    smem = pl.BlockSpec(memory_space=pltpu.SMEM)
    return pl.pallas_call(
        functools.partial(attend_kernel, head_size=head_size),
        grid=(steps,),
        in_specs=[smem, smem]
        + [column_block(rows, wide, part * steps) for part in range(3)]
        + [column_block(rows, wide, part * steps) for part in range(2)],
        out_specs=[column_block(rows, wide, 0), pl.BlockSpec((heads, rows), lambda step: (0, 0))],
        out_shape=[
            jax.ShapeDtypeStruct((rows, width), jnp.bfloat16),
            jax.ShapeDtypeStruct((heads, rows), jnp.float32),
        ],
        scratch_shapes=[pltpu.VMEM((2 * rows, rows), jnp.float32)],
        compiler_params=pltpu.CompilerParams(vmem_limit_bytes=40 << 20),
        cost_estimate=pl.CostEstimate(
            flops=16 * heads * rows * rows * head_size, bytes_accessed=12 * rows * width, transcendentals=2 * heads * rows * rows
        ),
        name="attend",
    )(place, slopes, qkv_rows, qkv_rows, qkv_rows, other_kv, other_kv)


def attend_back(qkv_rows, other_kv, grads, lse, place, slopes, head_size):
    rows, width = qkv_rows.shape[0], qkv_rows.shape[1] // 3
    wide = 2 * head_size
    steps = width // wide
    heads = width // head_size
    smem = pl.BlockSpec(memory_space=pltpu.SMEM)
    return pl.pallas_call(
        functools.partial(attend_back_kernel, head_size=head_size),
        grid=(steps,),
        in_specs=[smem, smem]
        + [column_block(rows, wide, part * steps) for part in range(3)]
        + [column_block(rows, wide, part * steps) for part in range(2)]
        + [column_block(rows, wide, 0), pl.BlockSpec((heads, rows), lambda step: (0, 0))],
        out_specs=[column_block(rows, wide, 0)] * 5,
        out_shape=[
            jax.ShapeDtypeStruct((rows, width), jnp.bfloat16),
            jax.ShapeDtypeStruct((rows, width), jnp.float32),
            jax.ShapeDtypeStruct((rows, width), jnp.float32),
            jax.ShapeDtypeStruct((rows, width), jnp.bfloat16),
            jax.ShapeDtypeStruct((rows, width), jnp.bfloat16),
        ],
        scratch_shapes=[pltpu.VMEM((2 * rows, rows), jnp.float32)],
        compiler_params=pltpu.CompilerParams(vmem_limit_bytes=40 << 20),
        cost_estimate=pl.CostEstimate(
            flops=40 * heads * rows * rows * head_size, bytes_accessed=24 * rows * width, transcendentals=2 * heads * rows * rows
        ),
        name="attend_back",
    )(place, slopes, qkv_rows, qkv_rows, qkv_rows, other_kv, other_kv, grads, lse)


def swap_pairs(size, step):
    return [(place, place ^ step) for place in range(size)]


def project_rows(left, right_t):
    return dot_nt(left, right_t)


def local_fast(
    tokens,
    prefix,
    cotangent,
    ln1_gain,
    ln1_bias,
    qkv_weight,
    qv_bias,
    out_weight,
    out_bias,
    ln2_gain,
    ln2_bias,
    up_weight,
    up_bias,
    down_weight,
    down_bias,
):
    low = jnp.bfloat16
    micros, _, tok_rows, width = tokens.shape
    heads, head_size = qv_bias.shape[1], qkv_weight.shape[3]
    inner = heads * head_size
    head_count = heads * lax.axis_size("mp")
    dp_size, seq_size = lax.axis_size("dp"), lax.axis_size("seq")
    parts = dp_size * seq_size
    shard = width // parts
    half_rows, half_width = tok_rows // 2, width // 2
    all_rows = micros * tok_rows
    dp_at, seq_at, mp_at = lax.axis_index("dp"), lax.axis_index("seq"), lax.axis_index("mp")
    core_at = mp_at % 2
    core_swap, chip_swap = swap_pairs(4, 1), swap_pairs(4, 2)
    seq_swap = swap_pairs(2, 1)

    def order_cols(values):
        split = values.reshape(values.shape[:-1] + (dp_size, 2, shard))
        first, second = split[..., 0, :], split[..., 1, :]
        own = jnp.where(seq_at == 0, first, second)
        other = jnp.where(seq_at == 0, second, first)
        flat = values.shape[:-1] + (half_width,)
        return jnp.concatenate([own.reshape(flat), other.reshape(flat)], axis=-1)

    def restore_cols(values):
        shape = values.shape[:-1] + (dp_size, shard)
        own = values[..., :half_width].reshape(shape)
        other = values[..., half_width:].reshape(shape)
        first = jnp.where(seq_at == 0, own, other)
        second = jnp.where(seq_at == 0, other, own)
        return jnp.stack([first, second], axis=-2).reshape(values.shape)

    def order_rows(values):
        split = values.reshape(micros, 2, half_rows, width)
        own = jnp.where(core_at == 0, split[:, 0], split[:, 1])
        other = jnp.where(core_at == 0, split[:, 1], split[:, 0])
        return jnp.stack([own, other], axis=1)

    def restore_rows(own, other):
        first = jnp.where(core_at == 0, own, other)
        second = jnp.where(core_at == 0, other, own)
        return jnp.concatenate([first, second], axis=0)

    packed = jnp.concatenate(
        [
            ln1_gain,
            ln1_bias,
            out_bias,
            ln2_gain,
            ln2_bias,
            down_bias,
            qv_bias.reshape(-1),
            up_bias.reshape(-1),
        ]
    )[None]
    for bit in range(2):
        arrived = lax.ppermute(packed, "dp", swap_pairs(4, 1 << bit))
        upper = (dp_at >> bit) & 1
        packed = jnp.where(
            upper == 0,
            jnp.concatenate([packed, arrived], axis=0),
            jnp.concatenate([arrived, packed], axis=0),
        )
    arrived = lax.ppermute(packed, "seq", seq_swap)
    packed = jnp.stack([packed, arrived])
    vectors = [
        packed[:, :, item * shard : (item + 1) * shard].reshape(width).astype(jnp.float32)
        for item in range(6)
    ]
    gain_one, bias_one, bias_out, gain_two, bias_two, bias_down = vectors
    natural = jnp.where(seq_at == 0, packed, packed[::-1]).transpose(1, 0, 2)
    first = 6 * shard
    qv_size = qv_bias.size
    qv_all = natural[:, :, first : first + qv_size].reshape(
        (parts,) + qv_bias.shape
    )
    qv_all = qv_all.transpose(1, 2, 0, 3).reshape(2, inner).astype(jnp.float32)
    up_all = natural[:, :, first + qv_size :].reshape((parts,) + up_bias.shape)
    up_shift = up_all.transpose(1, 0, 2).reshape(-1).astype(jnp.float32)
    qkv_shift = jnp.concatenate([qv_all[0], jnp.zeros((inner,), jnp.float32), qv_all[1]])

    ring = [dp * 2 for dp in range(dp_size)] + [dp * 2 + 1 for dp in reversed(range(dp_size))]
    onward = [(ring[place], ring[(place + 1) % parts]) for place in range(parts)]
    backward = [(there, here) for here, there in onward]
    ring_at = jnp.where(seq_at == 0, dp_at, parts - 1 - dp_at)
    qkv_own = qkv_weight.reshape(shard, 3 * inner)
    qkv_full = jnp.zeros((width, 3 * inner), low)

    def put(full, piece, place):
        piece_seq = place // dp_size
        piece_dp = jnp.where(piece_seq == 0, place, parts - 1 - place)
        slot = jnp.where(piece_seq == seq_at, 0, dp_size) + piece_dp
        return lax.dynamic_update_slice(full, piece, (slot * shard, 0))

    qkv_full = put(qkv_full, qkv_own, ring_at)
    ahead, behind = qkv_own, qkv_own
    for hop in range(1, parts // 2 + 1):
        ahead = lax.ppermute(ahead, ("dp", "seq"), onward)
        qkv_full = put(qkv_full, ahead, (ring_at - hop) % parts)
        if hop < parts // 2:
            behind = lax.ppermute(behind, ("dp", "seq"), backward)
            qkv_full = put(qkv_full, behind, (ring_at + hop) % parts)

    def gather(piece):
        own = lax.all_gather(piece, "dp", axis=0, tiled=True)
        return own, lax.ppermute(own, "seq", seq_swap)

    out_t = jnp.concatenate(gather(out_weight.reshape(inner, shard).T), axis=0)
    up_full = jnp.concatenate(gather(up_weight), axis=0)
    down_t = jnp.concatenate(gather(down_weight.T), axis=0)

    own_start = seq_at * tok_rows
    other_start = (1 - seq_at) * tok_rows
    flip = core_at * half_rows
    places = [
        jnp.stack([own_start, other_start, prefix[micro, 0], flip]).astype(jnp.int32)
        for micro in range(micros)
    ]
    head_numbers = mp_at * heads + jnp.arange(heads, dtype=jnp.int32) + 1
    slopes = jnp.exp2(-8.0 * head_numbers.astype(jnp.float32) / head_count) * log2e

    def reduce_half(own_part, other_part):
        arrived = lax.ppermute(other_part.astype(low), "mp", core_swap)
        pair = (own_part + arrived.astype(jnp.float32)).astype(low)
        across = lax.ppermute(pair, "mp", chip_swap)
        return pair.astype(jnp.float32) + across.astype(jnp.float32)

    def whole_rows(own_low):
        return jnp.concatenate([own_low, lax.ppermute(own_low, "mp", core_swap)], axis=0)

    ordered = order_rows(order_cols(tokens[:, 0]))
    cot = order_rows(order_cols(cotangent[:, 0]))
    cot_rows = cot.reshape(all_rows, width)
    h_one, _, _ = normalize(
        ordered.reshape(all_rows, width).astype(jnp.float32), gain_one, bias_one
    )
    h_one = h_one.astype(low)
    qkv = (dot_nn(h_one, qkv_full) + qkv_shift).astype(low)
    qkv_micro, other_kv = [], []
    for micro in range(micros):
        rows_here = qkv[micro * tok_rows : (micro + 1) * tok_rows]
        qkv_micro.append(rows_here)
        other_kv.append(lax.ppermute(rows_here[:, inner:], "seq", [(0, 1)]))
    attn, lse = [], []
    resid, normed_two, inv_two, h_two = [], [], [], []
    for micro in range(micros):
        attn_here, lse_here = attend(
            qkv_micro[micro], other_kv[micro], places[micro], slopes, head_size
        )
        attn.append(attn_here)
        lse.append(lse_here)
        branch = reduce_half(
            dot_nt(attn_here[:half_rows], out_t), dot_nt(attn_here[half_rows:], out_t)
        )
        resid_here = ordered[micro, 0].astype(jnp.float32) + branch + bias_out
        h_here, normed_here, inv_here = normalize(resid_here, gain_two, bias_two)
        resid.append(resid_here)
        normed_two.append(normed_here)
        inv_two.append(inv_here)
        h_two.append(whole_rows(h_here.astype(low)))
    attn = jnp.concatenate(attn, axis=0)
    h_two = jnp.concatenate(h_two, axis=0)
    up_pre = dot_nn(h_two, up_full) + up_shift
    cumulative = 0.5 * (1.0 + lax.erf(up_pre * inv_root_two))
    act = (up_pre * cumulative).astype(low)
    slope = (cumulative + up_pre * jnp.exp(-0.5 * up_pre * up_pre) * inv_root_tau).astype(low)

    def scatter(left, right):
        send = contract_rows(left[:, half_width:], right).astype(low)
        arrived = lax.ppermute(send, "seq", seq_swap)
        own = (contract_rows(left[:, :half_width], right) + arrived.astype(jnp.float32)).astype(low)
        return lax.psum_scatter(own, "dp", scatter_dimension=0, tiled=True)

    g_down_t = scatter(cot_rows, act)
    d_up = (dot_nn(cot_rows, down_t) * slope.astype(jnp.float32)).astype(low)
    g_up = scatter(h_two, d_up)
    sum_up = jnp.sum(d_up.astype(jnp.float32), axis=0)

    sum_gain_two, sum_bias_two, sum_out, sum_down = 0.0, 0.0, 0.0, 0.0
    d_resid, d_branch = [], []
    for micro in range(micros):
        base = micro * tok_rows
        d_h_two = reduce_half(
            dot_nt(d_up[base : base + half_rows], up_full),
            dot_nt(d_up[base + half_rows : base + tok_rows], up_full),
        )
        grad_here = cot[micro, 0].astype(jnp.float32)
        sum_gain_two += jnp.sum(d_h_two * normed_two[micro], axis=0)
        sum_bias_two += jnp.sum(d_h_two, axis=0)
        d_here = grad_here + normalize_back(d_h_two, normed_two[micro], inv_two[micro], gain_two)
        d_low = d_here.astype(low)
        sum_out += jnp.sum(d_low.astype(jnp.float32), axis=0)
        sum_down += jnp.sum(grad_here, axis=0)
        d_resid.append(d_here)
        d_branch.append(whole_rows(d_low))
    d_qkv = []
    for micro in range(micros):
        base = micro * tok_rows
        d_attn = dot_nn(d_branch[micro], out_t).astype(low)
        dq, dk, dv, dk_other, dv_other = attend_back(
            qkv_micro[micro], other_kv[micro], d_attn, lse[micro], places[micro], slopes, head_size
        )
        arrived = lax.ppermute(
            jnp.concatenate([dk_other, dv_other], axis=1), "seq", [(1, 0)]
        ).astype(jnp.float32)
        d_qkv.append(
            jnp.concatenate(
                [dq, (dk + arrived[:, :inner]).astype(low), (dv + arrived[:, inner:]).astype(low)],
                axis=1,
            )
        )
    d_branch = jnp.concatenate(d_branch, axis=0)
    g_out_t = scatter(d_branch, attn)
    d_qkv = jnp.concatenate(d_qkv, axis=0)
    g_qkv = scatter(h_one, d_qkv)
    sum_qkv = jnp.sum(d_qkv.astype(jnp.float32), axis=0)
    sum_qv = jnp.stack([sum_qkv[:inner], sum_qkv[2 * inner :]])

    sum_gain_one, sum_bias_one = 0.0, 0.0
    input_rows, output_rows = [], []
    for micro in range(micros):
        base = micro * tok_rows
        d_h_one = reduce_half(
            dot_nt(d_qkv[base : base + half_rows], qkv_full),
            dot_nt(d_qkv[base + half_rows : base + tok_rows], qkv_full),
        )
        _, normed_one, inv_one = normalize(
            ordered[micro, 0].astype(jnp.float32), gain_one, bias_one
        )
        sum_gain_one += jnp.sum(d_h_one * normed_one, axis=0)
        sum_bias_one += jnp.sum(d_h_one, axis=0)
        own = (d_resid[micro] + normalize_back(d_h_one, normed_one, inv_one, gain_one)).astype(low)
        own = restore_cols(own)
        input_rows.append(restore_rows(own, lax.ppermute(own, "mp", core_swap)))
        ffn = reduce_half(
            dot_nt(act[base : base + half_rows], down_t),
            dot_nt(act[base + half_rows : base + tok_rows], down_t),
        )
        own = restore_cols((resid[micro] + ffn + bias_down).astype(low))
        output_rows.append(restore_rows(own, lax.ppermute(own, "mp", core_swap)))

    feature_sums = jnp.stack(
        [sum_gain_one, sum_bias_one, sum_out, sum_gain_two, sum_bias_two, sum_down]
    )
    feature_sums = feature_sums + lax.ppermute(feature_sums, "mp", core_swap)
    features = feature_sums.reshape(6, 2, dp_size, shard).transpose(1, 2, 0, 3).reshape(2, dp_size, -1)
    qv_pieces = sum_qv.reshape(2, heads, dp_size, 2, -1).transpose(3, 2, 0, 1, 4)
    up_pieces = sum_up.reshape(-1, dp_size, 2, up_bias.shape[1]).transpose(2, 1, 0, 3)
    natural = jnp.concatenate(
        [qv_pieces.reshape(2, dp_size, -1), up_pieces.reshape(2, dp_size, -1)], axis=-1
    )
    natural = jnp.where(seq_at == 0, natural, natural[::-1])
    small = jnp.concatenate([features, natural], axis=-1)
    small = small[0] + lax.ppermute(small[1], "seq", seq_swap)
    for bit in range(2):
        small = small + lax.ppermute(small, "dp", swap_pairs(4, 1 << bit))
    small = lax.dynamic_slice_in_dim(small, dp_at, 1, axis=0)[0]
    vector_grads = [small[item * shard : (item + 1) * shard] for item in range(6)]
    qv_grad = small[first : first + qv_size].reshape(qv_bias.shape)
    up_bias_grad = small[first + qv_size :].reshape(up_bias.shape)
    wide = jnp.float32
    return (
        jnp.stack(output_rows)[:, None],
        jnp.stack(input_rows)[:, None],
        vector_grads[0],
        vector_grads[1],
        g_qkv.astype(wide).reshape(qkv_weight.shape),
        qv_grad,
        g_out_t.astype(wide).T.reshape(out_weight.shape),
        vector_grads[2],
        vector_grads[3],
        vector_grads[4],
        g_up.astype(wide),
        up_bias_grad,
        g_down_t.astype(wide).T,
        vector_grads[5],
    )


def local(
    tokens,
    prefix,
    cotangent,
    ln1_gain,
    ln1_bias,
    qkv_weight,
    qv_bias,
    out_weight,
    out_bias,
    ln2_gain,
    ln2_bias,
    up_weight,
    up_bias,
    down_weight,
    down_bias,
):
    gathered = (
        lax.all_gather(ln1_gain, ("dp", "seq"), axis=0, tiled=True),
        lax.all_gather(ln1_bias, ("dp", "seq"), axis=0, tiled=True),
        lax.all_gather(qkv_weight, ("dp", "seq"), axis=0, tiled=True),
        lax.all_gather(qv_bias, ("dp", "seq"), axis=2, tiled=True),
        lax.all_gather(out_weight, ("dp", "seq"), axis=2, tiled=True),
        lax.all_gather(out_bias, ("dp", "seq"), axis=0, tiled=True),
        lax.all_gather(ln2_gain, ("dp", "seq"), axis=0, tiled=True),
        lax.all_gather(ln2_bias, ("dp", "seq"), axis=0, tiled=True),
        lax.all_gather(up_weight, ("dp", "seq"), axis=0, tiled=True),
        lax.all_gather(up_bias, ("dp", "seq"), axis=1, tiled=True),
        lax.all_gather(down_weight, ("dp", "seq"), axis=1, tiled=True),
        lax.all_gather(down_bias, ("dp", "seq"), axis=0, tiled=True),
    )
    tok_rows = tokens.shape[2]
    feat_width = tokens.shape[3]
    seq_length = tok_rows * lax.axis_size("seq")
    heads_here = qv_bias.shape[1]
    head_size = qkv_weight.shape[3]
    head_count = heads_here * lax.axis_size("mp")
    inner = heads_here * head_size
    score_scale = head_size ** (-0.5)
    first_head = lax.axis_index("mp") * heads_here
    slopes = jnp.exp2(
        -8.0
        * (first_head + jnp.arange(heads_here, dtype=jnp.int32) + 1).astype(jnp.float32)
        / head_count
    )
    own_start = lax.axis_index("seq") * tok_rows
    query_pos = own_start + jnp.arange(tok_rows, dtype=jnp.int32)
    key_pos = jnp.arange(seq_length, dtype=jnp.int32)
    distance = jnp.abs(query_pos[:, None] - key_pos[None, :]).astype(jnp.float32)
    causal = key_pos[None, :] <= query_pos[:, None]
    gain_one = gathered[0].astype(jnp.float32)
    bias_one = gathered[1].astype(jnp.float32)
    qkv_flat = gathered[2].reshape(feat_width, 3 * inner)
    bias_qv = gathered[3].astype(jnp.float32).reshape(2, inner)
    qkv_shift = jnp.concatenate([bias_qv[0], jnp.zeros((inner,), jnp.float32), bias_qv[1]])
    out_flat = gathered[4].reshape(inner, feat_width)
    bias_out = gathered[5].astype(jnp.float32)
    gain_two = gathered[6].astype(jnp.float32)
    bias_two = gathered[7].astype(jnp.float32)
    up_mat = gathered[8]
    up_shift = gathered[9].astype(jnp.float32).reshape(-1)
    down_mat = gathered[10]
    bias_down = gathered[11].astype(jnp.float32)
    saved = []
    outputs = []
    for micro_idx in range(tokens.shape[0]):
        x_rows = tokens[micro_idx, 0].astype(jnp.float32)
        h_one, normed_one, inv_one = normalize(x_rows, gain_one, bias_one)
        h_one_low = h_one.astype(jnp.bfloat16)
        qkv_low = (
            jnp.dot(h_one_low, qkv_flat, preferred_element_type=jnp.float32) + qkv_shift
        ).astype(jnp.bfloat16)
        key_all, value_all = (
            lax.all_gather(qkv_low[:, inner : 2 * inner], "seq", axis=0, tiled=True),
            lax.all_gather(qkv_low[:, 2 * inner :], "seq", axis=0, tiled=True),
        )
        query_heads = split_heads(qkv_low[:, :inner], heads_here)
        key_heads = split_heads(key_all, heads_here)
        value_heads = split_heads(value_all, heads_here)
        visible = causal | (key_pos[None, :] < prefix[micro_idx, 0])

        def attend(head_item):
            queries, keys_h, values_h, slope_h = head_item
            scores = head_scores(queries, keys_h, slope_h, distance, visible, score_scale)
            row_max = jnp.max(scores, axis=-1, keepdims=True)
            exp_scores = jnp.exp(scores - row_max)
            row_total = jnp.sum(exp_scores, axis=-1, keepdims=True)
            attn_probs = exp_scores / row_total
            head_out = jnp.dot(
                attn_probs.astype(jnp.bfloat16), values_h, preferred_element_type=jnp.float32
            )
            return (head_out.astype(jnp.bfloat16), (row_max + jnp.log(row_total))[:, 0])

        head_outs, log_totals = lax.map(attend, (query_heads, key_heads, value_heads, slopes))
        attn_low = join_heads(head_outs)
        branch = (
            lax.psum(
                jnp.dot(attn_low, out_flat, preferred_element_type=jnp.float32).astype(
                    jnp.bfloat16
                ),
                "mp",
            ).astype(jnp.float32)
            + bias_out
        )
        resid = x_rows + branch
        h_two, normed_two, inv_two = normalize(resid, gain_two, bias_two)
        h_two_low = h_two.astype(jnp.bfloat16)
        up_pre = jnp.dot(h_two_low, up_mat, preferred_element_type=jnp.float32) + up_shift
        act_low = jax.nn.gelu(up_pre, approximate=False).astype(jnp.bfloat16)
        ffn_out = (
            lax.psum(
                jnp.dot(act_low, down_mat, preferred_element_type=jnp.float32).astype(jnp.bfloat16),
                "mp",
            ).astype(jnp.float32)
            + bias_down
        )
        outputs.append((resid + ffn_out).astype(jnp.bfloat16))
        saved.append(
            (
                normed_one,
                inv_one,
                h_one_low,
                query_heads,
                key_heads,
                value_heads,
                visible,
                log_totals,
                attn_low,
                normed_two,
                inv_two,
                h_two_low,
                up_pre,
                act_low,
            )
        )
    regathered = (
        lax.all_gather(ln1_gain, ("dp", "seq"), axis=0, tiled=True),
        lax.all_gather(ln1_bias, ("dp", "seq"), axis=0, tiled=True),
        lax.all_gather(qkv_weight, ("dp", "seq"), axis=0, tiled=True),
        lax.all_gather(qv_bias, ("dp", "seq"), axis=2, tiled=True),
        lax.all_gather(out_weight, ("dp", "seq"), axis=2, tiled=True),
        lax.all_gather(out_bias, ("dp", "seq"), axis=0, tiled=True),
        lax.all_gather(ln2_gain, ("dp", "seq"), axis=0, tiled=True),
        lax.all_gather(ln2_bias, ("dp", "seq"), axis=0, tiled=True),
        lax.all_gather(up_weight, ("dp", "seq"), axis=0, tiled=True),
        lax.all_gather(up_bias, ("dp", "seq"), axis=1, tiled=True),
        lax.all_gather(down_weight, ("dp", "seq"), axis=1, tiled=True),
        lax.all_gather(down_bias, ("dp", "seq"), axis=0, tiled=True),
    )
    back_gain_one = regathered[0].astype(jnp.float32)
    back_qkv = regathered[2].reshape(feat_width, 3 * inner)
    back_out = regathered[4].reshape(inner, feat_width)
    back_gain_two = regathered[6].astype(jnp.float32)
    back_up = regathered[8]
    back_down = regathered[10]
    up_bias_shape = regathered[9].shape
    running = None
    input_rows = []
    for micro_idx in range(tokens.shape[0]):
        (
            normed_one,
            inv_one,
            h_one_low,
            query_heads,
            key_heads,
            value_heads,
            visible,
            log_totals,
            attn_low,
            normed_two,
            inv_two,
            h_two_low,
            up_pre,
            act_low,
        ) = saved[micro_idx]
        grad_out = cotangent[micro_idx, 0]
        grad_full = grad_out.astype(jnp.float32)
        g_down_bias = jnp.sum(grad_full, axis=0)
        g_down = contract_rows(act_low, grad_out)
        d_up_low = (contract_cols(grad_out, back_down) * gelu_slope(up_pre)).astype(jnp.bfloat16)
        g_up_bias = jnp.sum(d_up_low.astype(jnp.float32), axis=0).reshape(up_bias_shape)
        g_up = contract_rows(h_two_low, d_up_low)
        d_h_two = lax.psum(contract_cols(d_up_low, back_up).astype(jnp.bfloat16), "mp").astype(
            jnp.float32
        )
        g_gain_two = jnp.sum(d_h_two * normed_two, axis=0)
        g_bias_two = jnp.sum(d_h_two, axis=0)
        d_resid = grad_full + normalize_back(d_h_two, normed_two, inv_two, back_gain_two)
        d_branch_low = d_resid.astype(jnp.bfloat16)
        g_out_bias = jnp.sum(d_branch_low.astype(jnp.float32), axis=0)
        g_out = contract_rows(attn_low, d_branch_low).reshape(heads_here, head_size, feat_width)
        d_attn_heads = split_heads(
            contract_cols(d_branch_low, back_out).astype(jnp.bfloat16), heads_here
        )

        def attend_back(head_item):
            queries, keys_h, values_h, grad_h, log_total, slope_h = head_item
            scores = head_scores(queries, keys_h, slope_h, distance, visible, score_scale)
            attn_probs = jnp.exp(scores - log_total[:, None])
            d_probs = contract_cols(grad_h, values_h)
            d_value = contract_rows(attn_probs.astype(jnp.bfloat16), grad_h)
            delta_sum = jnp.sum(d_probs * attn_probs, axis=-1, keepdims=True)
            d_scores = (attn_probs * (d_probs - delta_sum)).astype(jnp.bfloat16)
            d_query = jnp.dot(d_scores, keys_h, preferred_element_type=jnp.float32) * score_scale
            d_key = contract_rows(d_scores, queries) * score_scale
            return (d_query, d_key, d_value)

        d_query, d_key, d_value = lax.map(
            attend_back, (query_heads, key_heads, value_heads, d_attn_heads, log_totals, slopes)
        )
        key_rows, value_rows = (
            lax.psum_scatter(
                join_heads(d_key).astype(jnp.bfloat16), "seq", scatter_dimension=0, tiled=True
            ).astype(jnp.float32),
            lax.psum_scatter(
                join_heads(d_value).astype(jnp.bfloat16), "seq", scatter_dimension=0, tiled=True
            ).astype(jnp.float32),
        )
        query_low = join_heads(d_query).astype(jnp.bfloat16)
        value_low = value_rows.astype(jnp.bfloat16)
        d_qkv_low = jnp.concatenate([query_low, key_rows.astype(jnp.bfloat16), value_low], axis=1)
        g_qv_bias = jnp.stack(
            [
                jnp.sum(query_low.astype(jnp.float32), axis=0),
                jnp.sum(value_low.astype(jnp.float32), axis=0),
            ]
        ).reshape(2, heads_here, head_size)
        g_qkv = contract_rows(h_one_low, d_qkv_low).reshape(feat_width, 3, heads_here, head_size)
        d_h_one = lax.psum(contract_cols(d_qkv_low, back_qkv).astype(jnp.bfloat16), "mp").astype(
            jnp.float32
        )
        g_gain_one = jnp.sum(d_h_one * normed_one, axis=0)
        g_bias_one = jnp.sum(d_h_one, axis=0)
        input_rows.append(
            (d_resid + normalize_back(d_h_one, normed_one, inv_one, back_gain_one)).astype(
                jnp.bfloat16
            )
        )
        micro_grads = (
            g_gain_one,
            g_bias_one,
            g_qkv,
            g_qv_bias,
            g_out,
            g_out_bias,
            g_gain_two,
            g_bias_two,
            g_up,
            g_up_bias,
            g_down,
            g_down_bias,
        )
        if running is None:
            running = tuple(micro_grads)
        else:
            running = tuple(
                (total_arr + part_arr for total_arr, part_arr in zip(running, micro_grads))
            )
    running = (
        lax.psum_scatter(
            running[0].astype(jnp.bfloat16), ("dp", "seq"), scatter_dimension=0, tiled=True
        ).astype(jnp.float32),
        lax.psum_scatter(
            running[1].astype(jnp.bfloat16), ("dp", "seq"), scatter_dimension=0, tiled=True
        ).astype(jnp.float32),
        lax.psum_scatter(
            running[2].astype(jnp.bfloat16), ("dp", "seq"), scatter_dimension=0, tiled=True
        ).astype(jnp.float32),
        lax.psum_scatter(
            running[3].astype(jnp.bfloat16), ("dp", "seq"), scatter_dimension=2, tiled=True
        ).astype(jnp.float32),
        lax.psum_scatter(
            running[4].astype(jnp.bfloat16), ("dp", "seq"), scatter_dimension=2, tiled=True
        ).astype(jnp.float32),
        lax.psum_scatter(
            running[5].astype(jnp.bfloat16), ("dp", "seq"), scatter_dimension=0, tiled=True
        ).astype(jnp.float32),
        lax.psum_scatter(
            running[6].astype(jnp.bfloat16), ("dp", "seq"), scatter_dimension=0, tiled=True
        ).astype(jnp.float32),
        lax.psum_scatter(
            running[7].astype(jnp.bfloat16), ("dp", "seq"), scatter_dimension=0, tiled=True
        ).astype(jnp.float32),
        lax.psum_scatter(
            running[8].astype(jnp.bfloat16), ("dp", "seq"), scatter_dimension=0, tiled=True
        ).astype(jnp.float32),
        lax.psum_scatter(
            running[9].astype(jnp.bfloat16), ("dp", "seq"), scatter_dimension=1, tiled=True
        ).astype(jnp.float32),
        lax.psum_scatter(
            running[10].astype(jnp.bfloat16), ("dp", "seq"), scatter_dimension=1, tiled=True
        ).astype(jnp.float32),
        lax.psum_scatter(
            running[11].astype(jnp.bfloat16), ("dp", "seq"), scatter_dimension=0, tiled=True
        ).astype(jnp.float32),
    )
    output_rows = jnp.stack(outputs)[:, None]
    grad_rows = jnp.stack(input_rows)[:, None]
    return (
        output_rows,
        grad_rows,
        running[0],
        running[1],
        running[2],
        running[3],
        running[4],
        running[5],
        running[6],
        running[7],
        running[8],
        running[9],
        running[10],
        running[11],
    )


def solution(mesh):
    sizes = tuple(mesh.shape[axis] for axis in ("dp", "seq", "mp"))
    return jax.shard_map(
        local_fast if sizes == (4, 2, 4) else local,
        mesh=mesh,
        in_specs=(
            P(None, "dp", "seq", None),
            P(None, "dp"),
            P(None, "dp", "seq", None),
            P(("dp", "seq")),
            P(("dp", "seq")),
            P(("dp", "seq"), None, "mp", None),
            P(None, "mp", ("dp", "seq")),
            P("mp", None, ("dp", "seq")),
            P(("dp", "seq")),
            P(("dp", "seq")),
            P(("dp", "seq")),
            P(("dp", "seq"), "mp"),
            P("mp", ("dp", "seq")),
            P("mp", ("dp", "seq")),
            P(("dp", "seq")),
        ),
        out_specs=(
            P(None, "dp", "seq", None),
            P(None, "dp", "seq", None),
            P(("dp", "seq")),
            P(("dp", "seq")),
            P(("dp", "seq"), None, "mp", None),
            P(None, "mp", ("dp", "seq")),
            P("mp", None, ("dp", "seq")),
            P(("dp", "seq")),
            P(("dp", "seq")),
            P(("dp", "seq")),
            P(("dp", "seq"), "mp"),
            P("mp", ("dp", "seq")),
            P("mp", ("dp", "seq")),
            P(("dp", "seq")),
        ),
        check_vma=False,
    )
```

```python
import functools
import math

import jax
import jax.numpy as jnp
from jax import lax
from jax.experimental import pallas as pl
from jax.experimental.pallas import tpu as pltpu
from jax.sharding import PartitionSpec as P

eps_norm = 1e-05
masked_score = -1e30
inv_root_two = 0.7071067811865476
inv_root_tau = 0.3989422804014327


def contract_rows(left, right):
    return lax.dot_general(
        left, right, (((0,), (0,)), ((), ())), preferred_element_type=jnp.float32
    )


def contract_cols(left, right):
    return lax.dot_general(
        left, right, (((1,), (1,)), ((), ())), preferred_element_type=jnp.float32
    )


def normalize(values, gain_vec, shift_vec):
    row_mean = jnp.mean(values, axis=-1, keepdims=True)
    centered = values - row_mean
    variance = jnp.mean(centered * centered, axis=-1, keepdims=True)
    scale_inv = lax.rsqrt(variance + eps_norm)
    normed = centered * scale_inv
    return (normed * gain_vec + shift_vec, normed, scale_inv)


def normalize_back(grad_in, normed, scale_inv, gain_vec):
    scaled = grad_in * gain_vec
    return scale_inv * (
        scaled
        - jnp.mean(scaled, axis=-1, keepdims=True)
        - normed * jnp.mean(scaled * normed, axis=-1, keepdims=True)
    )


def gelu_slope(pre_act):
    cumulative = 0.5 * (1.0 + lax.erf(pre_act * inv_root_two))
    return cumulative + pre_act * jnp.exp(-0.5 * pre_act * pre_act) * inv_root_tau


def head_scores(queries, key_heads, slope_h, distance, visible, score_scale):
    raw_scores = contract_cols(queries, key_heads) * score_scale - slope_h * distance
    return jnp.where(visible, raw_scores, masked_score)


def split_heads(flat, count):
    return flat.reshape(flat.shape[0], count, -1).transpose(1, 0, 2)


def join_heads(stacked):
    return stacked.transpose(1, 0, 2).reshape(stacked.shape[1], -1)


log2e = math.log2(math.e)
hidden_distance = 1e30


def dot_nn(left, right):
    return lax.dot_general(
        left, right, (((1,), (0,)), ((), ())), preferred_element_type=jnp.float32
    )


def dot_nt(left, right):
    return lax.dot_general(
        left, right, (((1,), (1,)), ((), ())), preferred_element_type=jnp.float32
    )


times = {
    "enter": 4,
    "reorder": 5,
    "join": 6,
    "project": 10,
    "attend": 10,
    "out_shares": 3,
    "second_norm": 4,
    "expand": 22,
    "down_grad": 15,
    "expand_back": 15,
    "up_shares": 14,
    "up_grad": 14,
    "second_norm_back": 5,
    "attention_grad": 3,
    "attend_back": 17,
    "merge": 2,
    "out_grad": 5,
    "qkv_grad": 11,
    "qkv_shares": 11,
    "first_norm_back": 4,
    "down_shares": 14,
    "last_rows": 2,
    "restore": 20,
    "ring_add": 2,
}
bytes_per_time = 1000000
anywhere = pl.BlockSpec(memory_space=pl.ANY)


def fixed(step, *table):
    return (0, 0)


class Chain:
    last = None


def call(
    kernel, name, grid, in_specs, out_specs, out_shape, values, table=None, scratch=(), **more
):
    earlier = [] if Chain.last is None else [Chain.last]
    prefetched = 0 if table is None else 1
    first = len(in_specs) + prefetched
    count = len(earlier)

    def body(*refs):
        kernel(*refs[:first], *refs[first + count :])

    found = pl.pallas_call(
        body,
        grid_spec=pltpu.PrefetchScalarGridSpec(
            num_scalar_prefetch=prefetched,
            grid=grid,
            in_specs=list(in_specs) + [anywhere] * count,
            out_specs=out_specs,
            scratch_shapes=scratch,
        ),
        out_shape=out_shape,
        compiler_params=pltpu.CompilerParams(vmem_limit_bytes=50 << 20),
        cost_estimate=pl.CostEstimate(
            flops=0, bytes_accessed=times.get(name, 1) * bytes_per_time, transcendentals=0
        ),
        name=name,
        **more,
    )(*([] if table is None else [table]), *values, *earlier)
    Chain.last = found[0] if isinstance(found, (list, tuple)) else found
    return found


def array(shape, dtype=jnp.bfloat16):
    return jax.ShapeDtypeStruct(shape, dtype)


def dot_tn(left, right):
    return lax.dot_general(
        left, right, (((0,), (0,)), ((), ())), preferred_element_type=jnp.float32
    )


def error_function(values):
    bounded = jnp.clip(values, -3.832506856900711, 3.832506856900711)
    square = bounded * bounded
    above = jnp.full_like(square, 0.00022905065861350646)
    for factor in (
        0.0034082910107109506,
        0.050955695062380861,
        0.18520832239976145,
        1.128379143519084,
    ):
        above = above * square + factor
    below = jnp.full_like(square, -1.1791602954361697e-7)
    for factor in (
        0.000023547966471313185,
        0.0010179625278914885,
        0.014070470171167667,
        0.11098505178285362,
        0.49746925110067538,
        1.0,
    ):
        below = below * square + factor
    return bounded * above / below


def enter(values, gain_vec, bias_vec, core, half_rows):
    rows, width = values.shape

    def kernel(core_ref, values_ref, gain_ref, bias_ref, x_ref, h_ref):
        rows_low = values_ref[...]
        x_ref[...] = rows_low
        normed, _, _ = normalize(rows_low.astype(jnp.float32), gain_ref[...], bias_ref[...])
        h_ref[...] = normed.astype(h_ref.dtype)

    moved = pl.BlockSpec((half_rows, width), lambda step, core: (step ^ core[0], 0))
    whole = pl.BlockSpec((half_rows, width), lambda step, core: (step, 0))
    vector = pl.BlockSpec((1, width), fixed)
    return call(
        kernel,
        "enter",
        (rows // half_rows,),
        [moved, vector, vector],
        [whole, whole],
        [array((rows, width))] * 2,
        (values, gain_vec, bias_vec),
        core,
    )


def reorder(values, core, half_rows):
    rows, width = values.shape

    def kernel(core_ref, values_ref, out_ref):
        out_ref[...] = values_ref[...]

    return call(
        kernel,
        "reorder",
        (rows // half_rows,),
        [pl.BlockSpec((half_rows, width), lambda step, core: (step ^ core[0], 0))],
        pl.BlockSpec((half_rows, width), lambda step, core: (step, 0)),
        array((rows, width)),
        (values,),
        core,
    )


def restore(own, other, core, half_rows):
    micros, width = len(own), own[0].shape[1]

    def kernel(core_ref, *refs):
        out_ref = refs[-1]
        step = pl.program_id(0)
        mine = (step % 2) == core_ref[0]
        for micro in range(micros):
            here = step // 2 == micro

            @pl.when(here & mine)
            def _():
                out_ref[...] = refs[micro][...]

            @pl.when(here & jnp.logical_not(mine))
            def _():
                out_ref[...] = refs[micros + micro][...]

    piece = pl.BlockSpec((half_rows, width), fixed)
    return call(
        kernel,
        "restore",
        (2 * micros,),
        [pl.BlockSpec(memory_space=pltpu.SMEM)] + [piece] * (2 * micros),
        pl.BlockSpec((half_rows, width), lambda step: (step, 0)),
        array((2 * micros * half_rows, width)),
        (core, *own, *other),
    )


def pin(value):
    def kernel(*refs):
        pass

    return call(
        kernel,
        "pin",
        (1,),
        [anywhere],
        anywhere,
        array(value.shape, value.dtype),
        (value,),
        input_output_aliases={0: 0},
    )


def transpose_wide(values):
    rows, columns = values.shape

    def kernel(values_ref, out_ref):
        out_ref[...] = values_ref[...].T.astype(jnp.float32)

    return call(
        kernel,
        "transpose_wide",
        (4,),
        [pl.BlockSpec((rows, columns // 4), lambda step: (0, step))],
        pl.BlockSpec((columns // 4, rows), lambda step: (step, 0)),
        array((columns, rows), jnp.float32),
        (values,),
    )


def copy_wide(values):
    rows, columns = values.shape

    def kernel(values_ref, out_ref):
        out_ref[...] = values_ref[...].astype(jnp.float32)

    piece = pl.BlockSpec((rows // 4, columns), lambda step: (step, 0))
    return call(
        kernel,
        "copy_wide",
        (4,),
        [piece],
        piece,
        array((rows, columns), jnp.float32),
        (values,),
    )


def widen(own, arrived, upper):
    rows, columns = own.shape

    def kernel(upper_ref, own_ref, arrived_ref, out_ref):
        @pl.when(upper_ref[0] == 0)
        def _():
            out_ref[:rows, :] = own_ref[...]
            out_ref[rows:, :] = arrived_ref[...]

        @pl.when(upper_ref[0] != 0)
        def _():
            out_ref[:rows, :] = arrived_ref[...]
            out_ref[rows:, :] = own_ref[...]

    piece = pl.BlockSpec((rows, columns), fixed)
    return call(
        kernel,
        "widen",
        (1,),
        [pl.BlockSpec(memory_space=pltpu.SMEM), piece, piece],
        pl.BlockSpec((2 * rows, columns), fixed),
        array((2 * rows, columns), own.dtype),
        (upper, own, arrived),
    )


def far_halves(parts, table, item):
    rows, columns = parts.shape[0] // table.shape[0], parts.shape[1]
    half = pl.BlockSpec((rows // 2, columns), fixed)

    def kernel(table_ref, part_ref, top_ref, bottom_ref):
        top_ref[...] = part_ref[: rows // 2]
        bottom_ref[...] = part_ref[rows // 2 :]

    return call(
        kernel,
        "far_halves",
        (1,),
        [pl.BlockSpec((rows, columns), lambda step, table: (table[item], 0))],
        [half, half],
        [array((rows // 2, columns))] * 2,
        (parts,),
        table,
    )


def join(pieces, firsts):
    count = len(pieces)
    rows = sum(piece.shape[0] for piece in pieces)

    def kernel(firsts_ref, *refs):
        out_ref, sems = refs[count], refs[count + 1]
        copies = []
        for item in range(count):
            first = pl.multiple_of(firsts_ref[item], 128)
            target = out_ref.at[pl.ds(first, pieces[item].shape[0]), :]
            copies.append(pltpu.make_async_copy(refs[item], target, sems.at[item]))
        for copy in copies:
            copy.start()
        for copy in copies:
            copy.wait()

    return call(
        kernel,
        "join",
        (1,),
        [pl.BlockSpec(memory_space=pltpu.SMEM)] + [pl.BlockSpec(memory_space=pltpu.VMEM)] * count,
        anywhere,
        array((rows, pieces[0].shape[1])),
        (firsts, *pieces),
        scratch=[pltpu.SemaphoreType.DMA((count,))],
    )


def project(h_rows, weights, shift, inner):
    rows, width = h_rows.shape

    def kernel(h_ref, w_ref, shift_ref, q_ref, kv0_ref, kv1_ref):
        step = pl.program_id(0)
        low = (dot_nn(h_ref[...], w_ref[...]) + shift_ref[...]).astype(jnp.bfloat16)

        @pl.when(step == 0)
        def _():
            q_ref[...] = low

        @pl.when(step > 0)
        def _():
            kv0_ref[...] = low[: rows // 2]
            kv1_ref[...] = low[rows // 2 :]

    kv_spec = pl.BlockSpec((rows // 2, inner), lambda step: (0, jnp.maximum(step - 1, 0)))
    return call(
        kernel,
        "project",
        (3,),
        [
            pl.BlockSpec((rows, width), fixed),
            pl.BlockSpec((width, inner), lambda step: (0, step)),
            pl.BlockSpec((1, inner), lambda step: (0, step)),
        ],
        [pl.BlockSpec((rows, inner), fixed), kv_spec, kv_spec],
        [array((rows, inner)), array((rows // 2, 2 * inner)), array((rows // 2, 2 * inner))],
        (h_rows, weights, shift),
    )


def branch_shares(lefts, weights, columns, place, half_rows, tile, name):
    rows = sum(left.shape[0] for left in lefts)
    width = weights.shape[0]
    pairs = rows // (2 * half_rows)

    def kernel(*refs):
        left_refs, w_ref = refs[: len(lefts)], refs[len(lefts)]
        own_ref, other_ref = refs[-2:]
        at = 0
        for left_ref in left_refs:
            low = dot_nt(left_ref[...], w_ref[...]).astype(jnp.bfloat16)
            for half in range(left_ref.shape[0] // half_rows):
                pair, which = divmod(at, 2)
                target = own_ref if which == 0 else other_ref
                target[pair * half_rows : (pair + 1) * half_rows, :] = low[
                    half * half_rows : (half + 1) * half_rows
                ]
                at += 1

    out_spec = pl.BlockSpec((pairs * half_rows, tile), lambda step: (0, step))
    return call(
        kernel,
        name,
        (width // tile,),
        [pl.BlockSpec(left.shape, fixed) for left in lefts]
        + [pl.BlockSpec((tile, columns), lambda step: (step, place))],
        [out_spec, out_spec],
        [array((pairs * half_rows, width))] * 2,
        (*lefts, weights),
    )


def add_pair(own, arrived, micro, half_rows):
    width = own.shape[1]
    per_piece = arrived.shape[0] // half_rows
    rows = half_rows // 2

    def kernel(own_ref, arrived_ref, out_ref):
        total = own_ref[...].astype(jnp.float32) + arrived_ref[...].astype(jnp.float32)
        out_ref[...] = total.astype(out_ref.dtype)

    here = pl.BlockSpec((rows, width), lambda step: (2 * micro + step, 0))
    first = 2 * micro if per_piece > 1 else 0
    return call(
        kernel,
        "add_pair",
        (2,),
        [here, pl.BlockSpec((rows, width), lambda step: (first + step, 0))],
        pl.BlockSpec((rows, width), lambda step: (step, 0)),
        array((half_rows, width)),
        (own, arrived),
    )


def row_specs(half_rows, width, steps):
    rows = half_rows // steps
    here = pl.BlockSpec((rows, width), lambda step: (step, 0))
    vector = pl.BlockSpec((1, width), fixed)

    def at(micro):
        return pl.BlockSpec((rows, width), lambda step: (2 * micro * steps + step, 0))

    return here, vector, at


def second_norm(x_rows, pair, across, shift, gain_vec, bias_vec, micro, half_rows):
    width = x_rows.shape[1]
    here, vector, at = row_specs(half_rows, width, 4)

    def kernel(x_ref, pair_ref, across_ref, shift_ref, gain_ref, bias_ref, resid_ref, h_ref):
        branch = pair_ref[...].astype(jnp.float32) + across_ref[...].astype(jnp.float32)
        resid = x_ref[...].astype(jnp.float32) + (branch + shift_ref[...])
        resid_ref[...] = resid
        normed, _, _ = normalize(resid, gain_ref[...], bias_ref[...])
        h_ref[...] = normed.astype(h_ref.dtype)

    return call(
        kernel,
        "second_norm",
        (4,),
        [at(micro), here, here, vector, vector, vector],
        [here, here],
        [array((half_rows, width), jnp.float32), array((half_rows, width))],
        (x_rows, pair, across, shift, gain_vec, bias_vec),
    )


def expand(pieces, weights, shift, tile):
    rows = sum(piece.shape[0] for piece in pieces)
    width, hidden = weights.shape

    def kernel(*refs):
        piece_refs = refs[: len(pieces)]
        w_ref, shift_ref, act_ref, slope_ref, h_ref = refs[len(pieces) :]

        @pl.when(pl.program_id(0) == 0)
        def _():
            at = 0
            for piece in piece_refs:
                h_ref[at : at + piece.shape[0], :] = piece[...]
                at += piece.shape[0]

        up = dot_nn(h_ref[...], w_ref[...]) + shift_ref[...]
        cumulative = 0.5 * (1.0 + error_function(up * inv_root_two))
        act_ref[...] = (up * cumulative).astype(act_ref.dtype)
        density = jnp.exp(-0.5 * up * up) * inv_root_tau
        slope_ref[...] = (cumulative + up * density).astype(slope_ref.dtype)

    out_spec = pl.BlockSpec((rows, tile), lambda step: (0, step))
    return call(
        kernel,
        "expand",
        (hidden // tile,),
        [pl.BlockSpec(piece.shape, fixed) for piece in pieces]
        + [
            pl.BlockSpec((width, tile), lambda step: (0, step)),
            pl.BlockSpec((1, tile), lambda step: (0, step)),
        ],
        [out_spec, out_spec],
        [array((rows, hidden))] * 2,
        (*pieces, weights, shift),
        scratch=[pltpu.VMEM((rows, width), jnp.bfloat16)],
    )


def expand_back(grads, weights, slope, tile):
    rows, width = grads.shape
    hidden = weights.shape[1]

    def kernel(g_ref, w_ref, slope_ref, out_ref, sum_ref):
        low = (dot_nn(g_ref[...], w_ref[...]) * slope_ref[...].astype(jnp.float32)).astype(
            out_ref.dtype
        )
        out_ref[...] = low
        sum_ref[...] = jnp.sum(low.astype(jnp.float32), axis=0, keepdims=True)

    tile_spec = pl.BlockSpec((rows, tile), lambda step: (0, step))
    return call(
        kernel,
        "expand_back",
        (hidden // tile,),
        [
            pl.BlockSpec((rows, width), fixed),
            pl.BlockSpec((width, tile), lambda step: (0, step)),
            tile_spec,
        ],
        [tile_spec, pl.BlockSpec((1, tile), lambda step: (0, step))],
        [array((rows, hidden)), array((1, hidden), jnp.float32)],
        (grads, weights, slope),
    )


def weight_grad(lefts, rights, tile, name, whole=None, columns=None, place=0):
    width = lefts[0][0].shape[1]
    own_columns = rights[0][0].shape[1]
    columns = columns or own_columns

    def spec(piece, full):
        values, first, rows = piece
        if full:
            return pl.BlockSpec((rows, own_columns), lambda step: (first // rows, 0))
        return pl.BlockSpec((rows, tile), lambda step: (first // rows, step))

    def kernel(*refs):
        total = None
        for item in range(len(lefts)):
            part = dot_tn(refs[item][...], refs[len(lefts) + item][...])
            total = part if total is None else total + part
        refs[-1][...] = total.astype(refs[-1].dtype)

    values = [piece[0] for piece in (*lefts, *rights)]
    specs = [spec(piece, False) for piece in lefts] + [spec(piece, True) for piece in rights]
    more = {}
    if whole is not None:
        more["input_output_aliases"] = {len(values): 0}
        values.append(whole)
        specs.append(anywhere)
    return call(
        kernel,
        name,
        (width // tile,),
        specs,
        pl.BlockSpec((tile, own_columns), lambda step: (step, place)),
        array((width, columns)),
        values,
        **more,
    )


def second_norm_back(pair, across, resid, grads, gain_vec, micro, half_rows):
    width = resid.shape[1]
    here, vector, at = row_specs(half_rows, width, 4)

    def kernel(pair_ref, across_ref, resid_ref, g_ref, gain_ref, d_ref, low_ref, sum_ref):
        d_h = pair_ref[...].astype(jnp.float32) + across_ref[...].astype(jnp.float32)
        grad = g_ref[...].astype(jnp.float32)
        _, normed, scale_inv = normalize(resid_ref[...], gain_ref[...], 0.0)
        d_resid = grad + normalize_back(d_h, normed, scale_inv, gain_ref[...])
        low = d_resid.astype(low_ref.dtype)
        d_ref[...] = d_resid
        low_ref[...] = low

        @pl.when(pl.program_id(0) == 0)
        def _():
            sum_ref[...] = jnp.zeros_like(sum_ref)

        for item, value in enumerate((d_h * normed, d_h, low.astype(jnp.float32), grad)):
            sum_ref[item : item + 1, :] += jnp.sum(value, axis=0, keepdims=True)

    return call(
        kernel,
        "second_norm_back",
        (4,),
        [here, here, here, at(micro), vector],
        [here, here, pl.BlockSpec((4, width), fixed)],
        [
            array((half_rows, width), jnp.float32),
            array((half_rows, width)),
            array((4, width), jnp.float32),
        ],
        (pair, across, resid, grads, gain_vec),
    )


def attention_grad(pieces, weights, columns, place):
    rows = sum(piece.shape[0] for piece in pieces)
    width = weights.shape[0]

    def kernel(*refs):
        at = 0
        for piece in refs[: len(pieces)]:
            low = dot_nn(piece[...], refs[len(pieces)][...]).astype(jnp.bfloat16)
            refs[-1][at : at + piece.shape[0], :] = low
            at += piece.shape[0]

    return call(
        kernel,
        "attention_grad",
        (1,),
        [pl.BlockSpec(piece.shape, fixed) for piece in pieces]
        + [pl.BlockSpec((width, columns), lambda step: (0, place))],
        pl.BlockSpec((rows, columns), fixed),
        array((rows, columns)),
        (*pieces, weights),
    )


def merge(dq, dk, dv, more):
    rows, inner = dq.shape

    def kernel(dq_ref, dk_ref, dv_ref, more_ref, out_ref, sum_ref):
        low = out_ref.dtype
        parts = (
            dq_ref[...],
            (dk_ref[...] + more_ref[0].astype(jnp.float32)).astype(low),
            (dv_ref[...] + more_ref[1].astype(jnp.float32)).astype(low),
        )

        @pl.when(pl.program_id(0) == 0)
        def _():
            sum_ref[...] = jnp.zeros_like(sum_ref)

        for item, part in enumerate(parts):
            out_ref[:, item * inner : (item + 1) * inner] = part
            sum_ref[:, item * inner : (item + 1) * inner] += jnp.sum(
                part.astype(jnp.float32), axis=0, keepdims=True
            )

    piece = pl.BlockSpec((rows // 2, inner), lambda step: (step, 0))
    return call(
        kernel,
        "merge",
        (2,),
        [piece, piece, piece, pl.BlockSpec((2, rows // 2, inner), lambda step: (0, step, 0))],
        [
            pl.BlockSpec((rows // 2, 3 * inner), lambda step: (step, 0)),
            pl.BlockSpec((1, 3 * inner), fixed),
        ],
        [array((rows, 3 * inner)), array((1, 3 * inner), jnp.float32)],
        (dq, dk, dv, more),
    )


def first_norm_back(pair, across, x_rows, d_resid, gain_vec, micro, half_rows):
    width = x_rows.shape[1]
    here, vector, at = row_specs(half_rows, width, 4)

    def kernel(pair_ref, across_ref, x_ref, d_ref, gain_ref, out_ref, sum_ref):
        d_h = pair_ref[...].astype(jnp.float32) + across_ref[...].astype(jnp.float32)
        _, normed, scale_inv = normalize(x_ref[...].astype(jnp.float32), gain_ref[...], 0.0)
        total = d_ref[...] + normalize_back(d_h, normed, scale_inv, gain_ref[...])
        out_ref[...] = total.astype(out_ref.dtype)

        @pl.when(pl.program_id(0) == 0)
        def _():
            sum_ref[...] = jnp.zeros_like(sum_ref)

        for item, value in enumerate((d_h * normed, d_h)):
            sum_ref[item : item + 1, :] += jnp.sum(value, axis=0, keepdims=True)

    return call(
        kernel,
        "first_norm_back",
        (4,),
        [here, here, at(micro), here, vector],
        [here, pl.BlockSpec((2, width), fixed)],
        [array((half_rows, width)), array((2, width), jnp.float32)],
        (pair, across, x_rows, d_resid, gain_vec),
    )


def last_rows(resid, pair, across, shift):
    half_rows, width = resid.shape
    here, vector, _ = row_specs(half_rows, width, 4)

    def kernel(resid_ref, pair_ref, across_ref, shift_ref, out_ref):
        ffn = pair_ref[...].astype(jnp.float32) + across_ref[...].astype(jnp.float32)
        out_ref[...] = (resid_ref[...] + (ffn + shift_ref[...])).astype(out_ref.dtype)

    return call(
        kernel,
        "last_rows",
        (4,),
        [here, here, here, vector],
        here,
        array((half_rows, width)),
        (resid, pair, across, shift),
    )


def ring_add(parts, table, item, more, first=0, last=True):
    count = table.shape[0]
    rows, columns = parts.shape[0] // count, parts.shape[1]
    wide = jnp.float32

    def kernel(table_ref, part_ref, *refs):
        out_ref = refs[-1]
        total = part_ref[...].astype(wide)
        if more[0].shape[0] == rows:
            for value in refs[: len(more)]:
                total += value[...].astype(wide)
            out_ref[...] = total.astype(out_ref.dtype)
        else:
            out_ref[...] = total.astype(out_ref.dtype)
            half = more[0].shape[0]
            some = total[first : first + half] + refs[0][...].astype(wide)
            out_ref[first : first + half, :] = some.astype(out_ref.dtype)

    return call(
        kernel,
        "ring_add",
        (1,),
        [pl.BlockSpec((rows, columns), lambda step, table: (table[item], 0))]
        + [pl.BlockSpec(value.shape, fixed) for value in more],
        pl.BlockSpec((rows, columns), fixed),
        array((rows, columns), wide if last else jnp.bfloat16),
        (parts, *more),
        table,
    )


def fill_distance(place_ref, dist_ref, rows):
    own_first, other_first = place_ref[0], place_ref[1]
    prefix, flip = place_ref[2], place_ref[3]
    for block, first in enumerate((own_first, other_first)):
        shape = (rows, rows)
        key_pos = (lax.broadcasted_iota(jnp.int32, shape, 0) ^ flip) + first
        query_pos = (lax.broadcasted_iota(jnp.int32, shape, 1) ^ flip) + own_first
        visible = (key_pos <= query_pos) | (key_pos < prefix)
        gap = jnp.abs(query_pos - key_pos).astype(jnp.float32)
        dist_ref[block * rows : (block + 1) * rows, :] = jnp.where(visible, gap, hidden_distance)


def attend_kernel(place_ref, slope_ref, q_ref, k_ref, v_ref, ko_ref, vo_ref, out_ref, lse_ref, dist_ref, *, head_size):
    pair = pl.program_id(0)
    rows = q_ref.shape[0]

    @pl.when(pair == 0)
    def _():
        fill_distance(place_ref, dist_ref, rows)

    per_block = q_ref.shape[1] // head_size
    queries = q_ref[...]
    keys = jnp.concatenate([k_ref[...], ko_ref[...]], axis=0)
    values_t = jnp.concatenate([v_ref[...], vo_ref[...]], axis=0).T
    lane_head = lax.broadcasted_iota(jnp.int32, queries.shape, 1) // head_size
    parts = []
    for head in range(per_block):
        picked = jnp.where(lane_head == head, queries, jnp.zeros_like(queries))
        slope = slope_ref[pair * per_block + head]
        scores = dot_nt(keys, picked) * (log2e * head_size**-0.5) - dist_ref[...] * slope
        top = jnp.max(scores, axis=0, keepdims=True)
        weights = jnp.exp2(scores - top)
        total = jnp.sum(weights, axis=0, keepdims=True)
        head_out = dot_nn(values_t, weights.astype(jnp.bfloat16)) / total
        parts.append(head_out[head * head_size : (head + 1) * head_size])
        lse_ref[pl.ds(pair * per_block + head, 1), :] = top + jnp.log2(total)
    out_ref[...] = jnp.concatenate(parts, axis=0).T.astype(out_ref.dtype)


def attend_back_kernel(
    place_ref, slope_ref, q_ref, k_ref, v_ref, ko_ref, vo_ref, g_ref, lse_ref,
    dq_ref, dk_ref, dv_ref, other_ref, dist_ref, *, head_size
):
    pair = pl.program_id(0)
    rows = q_ref.shape[0]

    @pl.when(pair == 0)
    def _():
        fill_distance(place_ref, dist_ref, rows)

    per_block = q_ref.shape[1] // head_size
    queries, grads = q_ref[...], g_ref[...]
    keys = jnp.concatenate([k_ref[...], ko_ref[...]], axis=0)
    values = jnp.concatenate([v_ref[...], vo_ref[...]], axis=0)
    keys_t = keys.T
    lane_head = lax.broadcasted_iota(jnp.int32, queries.shape, 1) // head_size
    dq_parts = []
    d_keys, d_values = None, None
    for head in range(per_block):
        here = lane_head == head
        picked = jnp.where(here, queries, jnp.zeros_like(queries))
        picked_grad = jnp.where(here, grads, jnp.zeros_like(grads))
        slope = slope_ref[pair * per_block + head]
        scores = dot_nt(keys, picked) * (log2e * head_size**-0.5) - dist_ref[...] * slope
        probs = jnp.exp2(scores - lse_ref[pl.ds(pair * per_block + head, 1), :])
        weighted = dot_nt(values, picked_grad) * probs
        delta = jnp.sum(weighted, axis=0, keepdims=True)
        d_scores = (weighted - probs * delta).astype(jnp.bfloat16)
        value_part = dot_nn(probs.astype(jnp.bfloat16), picked_grad)
        key_part = dot_nn(d_scores, picked)
        d_values = value_part if d_values is None else d_values + value_part
        d_keys = key_part if d_keys is None else d_keys + key_part
        dq_part = dot_nn(keys_t, d_scores)
        dq_parts.append(dq_part[head * head_size : (head + 1) * head_size])
    scale = head_size**-0.5
    dq_ref[...] = (jnp.concatenate(dq_parts, axis=0).T * scale).astype(dq_ref.dtype)
    dk_ref[...] = (d_keys[:rows] * scale).astype(dk_ref.dtype)
    other_ref[0] = (d_keys[rows:] * scale).astype(other_ref.dtype)
    dv_ref[...] = d_values[:rows].astype(dv_ref.dtype)
    other_ref[1] = d_values[rows:].astype(other_ref.dtype)


def head_specs(queries, own_kv, head_size, micro):
    rows, inner = own_kv.shape[0], queries.shape[1]
    wide = 2 * head_size
    steps = inner // wide
    smem = pl.BlockSpec(memory_space=pltpu.SMEM)

    def at(first, row=0):
        return pl.BlockSpec((rows, wide), lambda step: (row, first + step))

    specs = [smem, smem, at(0, micro), at(0), at(steps), at(0), at(steps)]
    lse_spec = pl.BlockSpec((inner // head_size, rows), fixed)
    return rows, inner, steps, specs, at, lse_spec


def attend(queries, own_kv, other_kv, place, slopes, head_size, micro):
    rows, inner, steps, specs, at, lse_spec = head_specs(queries, own_kv, head_size, micro)
    return call(
        functools.partial(attend_kernel, head_size=head_size),
        "attend",
        (steps,),
        specs,
        [at(0), lse_spec],
        [array((rows, inner)), array((inner // head_size, rows), jnp.float32)],
        (place, slopes, queries, own_kv, own_kv, other_kv, other_kv),
        scratch=[pltpu.VMEM((2 * rows, rows), jnp.float32)],
    )


def attend_back(queries, own_kv, other_kv, grads, lse, place, slopes, head_size, micro):
    rows, inner, steps, specs, at, lse_spec = head_specs(queries, own_kv, head_size, micro)
    wide = 2 * head_size
    return call(
        functools.partial(attend_back_kernel, head_size=head_size),
        "attend_back",
        (steps,),
        specs + [at(0), lse_spec],
        [at(0), at(0), at(0), pl.BlockSpec((2, rows, wide), lambda step: (0, 0, step))],
        [
            array((rows, inner)),
            array((rows, inner), jnp.float32),
            array((rows, inner), jnp.float32),
            array((2, rows, inner)),
        ],
        (place, slopes, queries, own_kv, own_kv, other_kv, other_kv, grads, lse),
        scratch=[pltpu.VMEM((2 * rows, rows), jnp.float32)],
    )


def ring_places(dp_size, seq_size):
    places = []
    for seq in range(seq_size):
        line = range(dp_size) if seq % 2 == 0 else reversed(range(dp_size))
        places += [dp * seq_size + seq for dp in line]
    return places


def swap_pairs(size, step):
    return [(place, place ^ step) for place in range(size)]


class RingGather:
    def __init__(self, piece, table, ways):
        self.blocks, self.ways = table.shape[0], ways
        self.firsts = table * piece.shape[0]
        self.found, self.places = [piece], [self.firsts[0]]
        self.pair, self.hop = (piece, piece), 0

    def step(self):
        half = self.blocks // 2
        ahead, behind = self.pair
        middle = ahead.shape[0] // 2
        if self.hop > 0:
            ahead, behind = pin(ahead), pin(behind)
            self.found += [ahead, behind]
            self.places += [self.firsts[self.blocks - self.hop], self.firsts[self.hop]]
        self.hop += 1
        if self.hop == half:
            ahead, behind = ahead[:middle], behind[middle:]
            self.places += [self.firsts[half], self.firsts[half] + middle]
        self.pair = (
            lax.ppermute(ahead, ("dp", "seq"), self.ways[0]),
            lax.ppermute(behind, ("dp", "seq"), self.ways[1]),
        )

    def whole(self):
        return join([*self.found, *self.pair], jnp.stack(self.places).astype(jnp.int32))


class RingScatter:
    def __init__(self, parts, table, ways):
        self.parts, self.table, self.ways = parts, table, ways
        self.blocks = table.shape[0]
        self.rows = parts.shape[0] // self.blocks
        self.pair, self.hop = None, 0

    def step(self):
        half, middle = self.blocks // 2, self.rows // 2
        if self.hop == 0:
            ahead, behind = far_halves(self.parts, self.table, half)
        else:
            ahead, behind = (
                ring_add(self.parts, self.table, half + way * self.hop, [value], first, False)
                for way, value, first in ((-1, self.pair[0], 0), (1, self.pair[1], middle))
            )
        self.pair = (
            lax.ppermute(ahead, ("dp", "seq"), self.ways[0]),
            lax.ppermute(behind, ("dp", "seq"), self.ways[1]),
        )
        self.hop += 1

    def total(self):
        return ring_add(self.parts, self.table, 0, list(self.pair))


def local_fast(
    tokens,
    prefix,
    cotangent,
    ln1_gain,
    ln1_bias,
    qkv_weight,
    qv_bias,
    out_weight,
    out_bias,
    ln2_gain,
    ln2_bias,
    up_weight,
    up_bias,
    down_weight,
    down_bias,
):
    Chain.last = None
    low, wide = jnp.bfloat16, jnp.float32
    micros, _, tok_rows, width = tokens.shape
    heads, head_size = qv_bias.shape[1], qkv_weight.shape[3]
    inner = heads * head_size
    head_count = heads * lax.axis_size("mp")
    dp_size, seq_size = lax.axis_size("dp"), lax.axis_size("seq")
    blocks = dp_size * seq_size
    shard = width // blocks
    half_rows = tok_rows // 2
    all_rows = micros * tok_rows
    dp_at, seq_at, mp_at = lax.axis_index("dp"), lax.axis_index("seq"), lax.axis_index("mp")
    core_at = mp_at % 2
    core_swap, chip_swap = swap_pairs(4, 1), swap_pairs(4, 2)

    ring = ring_places(dp_size, seq_size)
    onward = [(ring[place], ring[(place + 1) % blocks]) for place in range(blocks)]
    backward = [(there, here) for here, there in onward]
    ways = (onward, backward)
    ring_at = jnp.where(seq_at == 0, dp_at, blocks - 1 - dp_at).astype(jnp.int32)
    along = (ring_at + jnp.arange(blocks, dtype=jnp.int32)) % blocks
    table = jnp.where(along < dp_size, along, blocks - 1 - along) * seq_size + along // dp_size
    table = table.astype(jnp.int32)
    core = core_at.astype(jnp.int32)[None]

    places = [
        jnp.stack(
            [
                seq_at * tok_rows,
                (1 - seq_at) * tok_rows,
                prefix[micro, 0],
                core_at * half_rows,
            ]
        ).astype(jnp.int32)
        for micro in range(micros)
    ]
    head_numbers = mp_at * heads + jnp.arange(heads, dtype=jnp.int32) + 1
    slopes = jnp.exp2(-8.0 * head_numbers.astype(wide) / head_count) * log2e

    def reduce_share(own, arrived, micro):
        pair = add_pair(own, arrived, micro, half_rows)
        return pair, lax.ppermute(pair, "mp", chip_swap)

    def scatter(parts):
        return lax.psum_scatter(parts, ("dp", "seq"), scatter_dimension=0, tiled=True)

    def swap_cores(values):
        return lax.ppermute(values, "mp", core_swap)

    small_parts = (ln1_gain, ln1_bias, out_bias, ln2_gain, ln2_bias, down_bias, qv_bias, up_bias)
    packed = jnp.concatenate([part.reshape(-1) for part in small_parts]).astype(wide)[None]
    packed = pin(packed)
    arrived = lax.ppermute(packed, "seq", swap_pairs(2, 1))
    attention_ring = RingGather(
        pin(
            jnp.concatenate(
                [qkv_weight.reshape(shard, 3 * inner), out_weight.reshape(inner, shard).T], axis=1
            )
        ),
        table,
        ways,
    )
    attention_ring.step()
    packed = widen(packed, arrived, seq_at.astype(jnp.int32)[None])
    arrived = lax.ppermute(packed, "dp", swap_pairs(4, 1))
    attention_ring.step()
    packed = widen(packed, arrived, (dp_at & 1).astype(jnp.int32)[None])
    arrived = lax.ppermute(packed, "dp", swap_pairs(4, 2))
    attention_ring.step()
    cot_rows = reorder(cotangent.reshape(all_rows, width), core, half_rows)
    packed = widen(packed, arrived, (dp_at >> 1).astype(jnp.int32)[None])
    attention_ring.step()
    gain_one, bias_one, bias_out, gain_two, bias_two, bias_down = [
        packed[:, item * shard : (item + 1) * shard].reshape(1, width) for item in range(6)
    ]
    first = 6 * shard
    qv_size = qv_bias.size
    qv_all = packed[:, first : first + qv_size].reshape((blocks,) + qv_bias.shape)
    qv_all = qv_all.transpose(1, 2, 0, 3).reshape(2, inner)
    up_all = packed[:, first + qv_size :].reshape((blocks,) + up_bias.shape)
    up_shift = up_all.transpose(1, 0, 2).reshape(1, -1)
    qkv_shift = jnp.concatenate([qv_all[0], jnp.zeros((inner,), wide), qv_all[1]])[None]
    x_rows, h_one = enter(tokens.reshape(all_rows, width), gain_one, bias_one, core, half_rows)
    attention_full = attention_ring.whole()
    queries, *own_kv = project(h_one, attention_full, qkv_shift, inner)
    other_kv = [lax.ppermute(value, "seq", [(0, 1)]) for value in own_kv]

    attn, lse = [], []
    for micro in range(micros):
        attn_here, lse_here = attend(
            queries, own_kv[micro], other_kv[micro], places[micro], slopes, head_size, micro
        )
        attn.append(attn_here)
        lse.append(lse_here)
        if micro == 0:
            up_ring = RingGather(pin(up_weight), table, ways)
            up_ring.step()
    own, other = branch_shares(attn, attention_full, inner, 3, half_rows, 512, "out_shares")
    arrived = swap_cores(other)
    shares = [reduce_share(own, arrived, micro) for micro in range(micros)]
    up_ring.step()
    up_ring.step()
    resid, h_two = [], []
    for micro in range(micros):
        resid_here, h_here = second_norm(
            x_rows, *shares[micro], bias_out, gain_two, bias_two, micro, half_rows
        )
        resid.append(resid_here)
        h_two += [h_here, swap_cores(h_here)]
        if micro == 0:
            up_ring.step()
            down_ring = RingGather(pin(down_weight.T), table, ways)
            down_ring.step()
    up_full = up_ring.whole()
    down_ring.step()
    act, slope = expand(h_two, up_full, up_shift, 256)
    down_ring.step()
    down_parts = weight_grad([(cot_rows, 0, all_rows)], [(act, 0, all_rows)], 256, "down_grad")
    down_ring.step()
    g_down_t = scatter(pin(down_parts))
    down_t = down_ring.whole()
    d_up, sum_up = expand_back(cot_rows, down_t, slope, 256)
    own, other = branch_shares([d_up], up_full, d_up.shape[1], 0, half_rows, 256, "up_shares")
    arrived = swap_cores(other)
    shares = [reduce_share(own, arrived, micro) for micro in range(micros)]
    ffn_own, other = branch_shares([act], down_t, act.shape[1], 0, half_rows, 256, "down_shares")
    ffn_arrived = swap_cores(other)

    norm_sums, d_resid, d_branch, backs = 0.0, [], [], []
    d_qkv, sum_qkv, output_rows = [], 0.0, []
    for micro in range(micros):
        d_here, d_low, sums = second_norm_back(
            *shares[micro], resid[micro], cot_rows, gain_two, micro, half_rows
        )
        norm_sums += sums
        d_resid.append(d_here)
        d_branch += [d_low, swap_cores(d_low)]
        d_attn = attention_grad(d_branch[-2:], attention_full, inner, 3)
        dq, dk, dv, more = attend_back(
            queries,
            own_kv[micro],
            other_kv[micro],
            d_attn,
            lse[micro],
            places[micro],
            slopes,
            head_size,
            micro,
        )
        backs.append((dq, dk, dv, lax.ppermute(more, "seq", [(1, 0)])))
    d_here, sums = merge(*backs[0])
    d_qkv.append(d_here)
    sum_qkv += sums[0]
    up_parts = weight_grad(
        [(piece, 0, half_rows) for piece in h_two],
        [(d_up, item * half_rows, half_rows) for item in range(2 * micros)],
        256,
        "up_grad",
    )
    g_up = scatter(up_parts)
    ring_columns = attention_full.shape[1]
    out_parts = weight_grad(
        [(piece, 0, half_rows) for piece in d_branch],
        [(value, half * half_rows, half_rows) for value in attn for half in range(2)],
        512,
        "out_grad",
        columns=ring_columns,
        place=3,
    )
    shares = [reduce_share(ffn_own, ffn_arrived, micro) for micro in range(micros)]
    d_here, sums = merge(*backs[1])
    d_qkv.append(d_here)
    sum_qkv += sums[0]
    attention_parts = weight_grad(
        [(h_one, micro * tok_rows, tok_rows) for micro in range(micros)],
        [(value, 0, tok_rows) for value in d_qkv],
        256,
        "qkv_grad",
        whole=out_parts,
        columns=ring_columns,
    )
    attention_grads = RingScatter(attention_parts, table, ways)
    attention_grads.step()
    for micro in range(micros):
        output_rows.append(last_rows(resid[micro], *shares[micro], bias_down))
    output_other = [swap_cores(piece) for piece in output_rows]
    attention_grads.step()
    own, other = branch_shares(
        d_qkv, attention_full, 3 * inner, 0, half_rows, 256, "qkv_shares"
    )
    arrived = swap_cores(other)
    output = restore(output_rows, output_other, core, half_rows)
    g_down_wide = transpose_wide(g_down_t)
    shares = [reduce_share(own, arrived, micro) for micro in range(micros)]
    first_sums, input_rows = 0.0, []
    for micro in range(micros):
        rows_here, sums = first_norm_back(
            *shares[micro], x_rows, d_resid[micro], gain_one, micro, half_rows
        )
        first_sums += sums
        input_rows.append(rows_here)
    input_other = [swap_cores(piece) for piece in input_rows]
    attention_grads.step()
    attention_grads.step()
    g_up_wide = copy_wide(g_up)
    input_grad = restore(input_rows, input_other, core, half_rows)
    g_attention = attention_grads.total()
    sum_qv = jnp.stack([sum_qkv[:inner], sum_qkv[2 * inner :]])

    feature_sums = jnp.stack(
        [first_sums[0], first_sums[1], norm_sums[2], norm_sums[0], norm_sums[1], norm_sums[3]]
    )
    feature_sums = feature_sums + lax.ppermute(feature_sums, "mp", core_swap)
    features = feature_sums.reshape(6, blocks, shard).transpose(1, 0, 2).reshape(blocks, -1)
    qv_pieces = sum_qv.reshape(2, heads, blocks, -1).transpose(2, 0, 1, 3)
    up_pieces = sum_up.reshape(-1, blocks, up_bias.shape[1]).transpose(1, 0, 2)
    small = jnp.concatenate(
        [features, qv_pieces.reshape(blocks, -1), up_pieces.reshape(blocks, -1)], axis=-1
    ).reshape(dp_size, seq_size, -1)
    own = jnp.where(seq_at == 0, small[:, 0], small[:, 1])
    other = jnp.where(seq_at == 0, small[:, 1], small[:, 0])
    small = own + lax.ppermute(other, "seq", swap_pairs(2, 1))
    for bit in range(2):
        small = small + lax.ppermute(small, "dp", swap_pairs(4, 1 << bit))
    small = lax.dynamic_slice_in_dim(small, dp_at, 1, axis=0)[0]
    vector_grads = [small[item * shard : (item + 1) * shard] for item in range(6)]
    qv_grad = small[first : first + qv_size].reshape(qv_bias.shape)
    up_bias_grad = small[first + qv_size :].reshape(up_bias.shape)
    return (
        output.reshape(tokens.shape),
        input_grad.reshape(tokens.shape),
        vector_grads[0],
        vector_grads[1],
        g_attention[:, : 3 * inner].reshape(qkv_weight.shape),
        qv_grad,
        g_attention[:, 3 * inner :].T.reshape(out_weight.shape),
        vector_grads[2],
        vector_grads[3],
        vector_grads[4],
        g_up_wide,
        up_bias_grad,
        g_down_wide,
        vector_grads[5],
    )


def local(
    tokens,
    prefix,
    cotangent,
    ln1_gain,
    ln1_bias,
    qkv_weight,
    qv_bias,
    out_weight,
    out_bias,
    ln2_gain,
    ln2_bias,
    up_weight,
    up_bias,
    down_weight,
    down_bias,
):
    gathered = (
        lax.all_gather(ln1_gain, ("dp", "seq"), axis=0, tiled=True),
        lax.all_gather(ln1_bias, ("dp", "seq"), axis=0, tiled=True),
        lax.all_gather(qkv_weight, ("dp", "seq"), axis=0, tiled=True),
        lax.all_gather(qv_bias, ("dp", "seq"), axis=2, tiled=True),
        lax.all_gather(out_weight, ("dp", "seq"), axis=2, tiled=True),
        lax.all_gather(out_bias, ("dp", "seq"), axis=0, tiled=True),
        lax.all_gather(ln2_gain, ("dp", "seq"), axis=0, tiled=True),
        lax.all_gather(ln2_bias, ("dp", "seq"), axis=0, tiled=True),
        lax.all_gather(up_weight, ("dp", "seq"), axis=0, tiled=True),
        lax.all_gather(up_bias, ("dp", "seq"), axis=1, tiled=True),
        lax.all_gather(down_weight, ("dp", "seq"), axis=1, tiled=True),
        lax.all_gather(down_bias, ("dp", "seq"), axis=0, tiled=True),
    )
    tok_rows = tokens.shape[2]
    feat_width = tokens.shape[3]
    seq_length = tok_rows * lax.axis_size("seq")
    heads_here = qv_bias.shape[1]
    head_size = qkv_weight.shape[3]
    head_count = heads_here * lax.axis_size("mp")
    inner = heads_here * head_size
    score_scale = head_size ** (-0.5)
    first_head = lax.axis_index("mp") * heads_here
    slopes = jnp.exp2(
        -8.0
        * (first_head + jnp.arange(heads_here, dtype=jnp.int32) + 1).astype(jnp.float32)
        / head_count
    )
    own_start = lax.axis_index("seq") * tok_rows
    query_pos = own_start + jnp.arange(tok_rows, dtype=jnp.int32)
    key_pos = jnp.arange(seq_length, dtype=jnp.int32)
    distance = jnp.abs(query_pos[:, None] - key_pos[None, :]).astype(jnp.float32)
    causal = key_pos[None, :] <= query_pos[:, None]
    gain_one = gathered[0].astype(jnp.float32)
    bias_one = gathered[1].astype(jnp.float32)
    qkv_flat = gathered[2].reshape(feat_width, 3 * inner)
    bias_qv = gathered[3].astype(jnp.float32).reshape(2, inner)
    qkv_shift = jnp.concatenate([bias_qv[0], jnp.zeros((inner,), jnp.float32), bias_qv[1]])
    out_flat = gathered[4].reshape(inner, feat_width)
    bias_out = gathered[5].astype(jnp.float32)
    gain_two = gathered[6].astype(jnp.float32)
    bias_two = gathered[7].astype(jnp.float32)
    up_mat = gathered[8]
    up_shift = gathered[9].astype(jnp.float32).reshape(-1)
    down_mat = gathered[10]
    bias_down = gathered[11].astype(jnp.float32)
    saved = []
    outputs = []
    for micro_idx in range(tokens.shape[0]):
        x_rows = tokens[micro_idx, 0].astype(jnp.float32)
        h_one, normed_one, inv_one = normalize(x_rows, gain_one, bias_one)
        h_one_low = h_one.astype(jnp.bfloat16)
        qkv_low = (
            jnp.dot(h_one_low, qkv_flat, preferred_element_type=jnp.float32) + qkv_shift
        ).astype(jnp.bfloat16)
        key_all, value_all = (
            lax.all_gather(qkv_low[:, inner : 2 * inner], "seq", axis=0, tiled=True),
            lax.all_gather(qkv_low[:, 2 * inner :], "seq", axis=0, tiled=True),
        )
        query_heads = split_heads(qkv_low[:, :inner], heads_here)
        key_heads = split_heads(key_all, heads_here)
        value_heads = split_heads(value_all, heads_here)
        visible = causal | (key_pos[None, :] < prefix[micro_idx, 0])

        def attend(head_item):
            queries, keys_h, values_h, slope_h = head_item
            scores = head_scores(queries, keys_h, slope_h, distance, visible, score_scale)
            row_max = jnp.max(scores, axis=-1, keepdims=True)
            exp_scores = jnp.exp(scores - row_max)
            row_total = jnp.sum(exp_scores, axis=-1, keepdims=True)
            attn_probs = exp_scores / row_total
            head_out = jnp.dot(
                attn_probs.astype(jnp.bfloat16), values_h, preferred_element_type=jnp.float32
            )
            return (head_out.astype(jnp.bfloat16), (row_max + jnp.log(row_total))[:, 0])

        head_outs, log_totals = lax.map(attend, (query_heads, key_heads, value_heads, slopes))
        attn_low = join_heads(head_outs)
        branch = (
            lax.psum(
                jnp.dot(attn_low, out_flat, preferred_element_type=jnp.float32).astype(
                    jnp.bfloat16
                ),
                "mp",
            ).astype(jnp.float32)
            + bias_out
        )
        resid = x_rows + branch
        h_two, normed_two, inv_two = normalize(resid, gain_two, bias_two)
        h_two_low = h_two.astype(jnp.bfloat16)
        up_pre = jnp.dot(h_two_low, up_mat, preferred_element_type=jnp.float32) + up_shift
        act_low = jax.nn.gelu(up_pre, approximate=False).astype(jnp.bfloat16)
        ffn_out = (
            lax.psum(
                jnp.dot(act_low, down_mat, preferred_element_type=jnp.float32).astype(jnp.bfloat16),
                "mp",
            ).astype(jnp.float32)
            + bias_down
        )
        outputs.append((resid + ffn_out).astype(jnp.bfloat16))
        saved.append(
            (
                normed_one,
                inv_one,
                h_one_low,
                query_heads,
                key_heads,
                value_heads,
                visible,
                log_totals,
                attn_low,
                normed_two,
                inv_two,
                h_two_low,
                up_pre,
                act_low,
            )
        )
    regathered = (
        lax.all_gather(ln1_gain, ("dp", "seq"), axis=0, tiled=True),
        lax.all_gather(ln1_bias, ("dp", "seq"), axis=0, tiled=True),
        lax.all_gather(qkv_weight, ("dp", "seq"), axis=0, tiled=True),
        lax.all_gather(qv_bias, ("dp", "seq"), axis=2, tiled=True),
        lax.all_gather(out_weight, ("dp", "seq"), axis=2, tiled=True),
        lax.all_gather(out_bias, ("dp", "seq"), axis=0, tiled=True),
        lax.all_gather(ln2_gain, ("dp", "seq"), axis=0, tiled=True),
        lax.all_gather(ln2_bias, ("dp", "seq"), axis=0, tiled=True),
        lax.all_gather(up_weight, ("dp", "seq"), axis=0, tiled=True),
        lax.all_gather(up_bias, ("dp", "seq"), axis=1, tiled=True),
        lax.all_gather(down_weight, ("dp", "seq"), axis=1, tiled=True),
        lax.all_gather(down_bias, ("dp", "seq"), axis=0, tiled=True),
    )
    back_gain_one = regathered[0].astype(jnp.float32)
    back_qkv = regathered[2].reshape(feat_width, 3 * inner)
    back_out = regathered[4].reshape(inner, feat_width)
    back_gain_two = regathered[6].astype(jnp.float32)
    back_up = regathered[8]
    back_down = regathered[10]
    up_bias_shape = regathered[9].shape
    running = None
    input_rows = []
    for micro_idx in range(tokens.shape[0]):
        (
            normed_one,
            inv_one,
            h_one_low,
            query_heads,
            key_heads,
            value_heads,
            visible,
            log_totals,
            attn_low,
            normed_two,
            inv_two,
            h_two_low,
            up_pre,
            act_low,
        ) = saved[micro_idx]
        grad_out = cotangent[micro_idx, 0]
        grad_full = grad_out.astype(jnp.float32)
        g_down_bias = jnp.sum(grad_full, axis=0)
        g_down = contract_rows(act_low, grad_out)
        d_up_low = (contract_cols(grad_out, back_down) * gelu_slope(up_pre)).astype(jnp.bfloat16)
        g_up_bias = jnp.sum(d_up_low.astype(jnp.float32), axis=0).reshape(up_bias_shape)
        g_up = contract_rows(h_two_low, d_up_low)
        d_h_two = lax.psum(contract_cols(d_up_low, back_up).astype(jnp.bfloat16), "mp").astype(
            jnp.float32
        )
        g_gain_two = jnp.sum(d_h_two * normed_two, axis=0)
        g_bias_two = jnp.sum(d_h_two, axis=0)
        d_resid = grad_full + normalize_back(d_h_two, normed_two, inv_two, back_gain_two)
        d_branch_low = d_resid.astype(jnp.bfloat16)
        g_out_bias = jnp.sum(d_branch_low.astype(jnp.float32), axis=0)
        g_out = contract_rows(attn_low, d_branch_low).reshape(heads_here, head_size, feat_width)
        d_attn_heads = split_heads(
            contract_cols(d_branch_low, back_out).astype(jnp.bfloat16), heads_here
        )

        def attend_back(head_item):
            queries, keys_h, values_h, grad_h, log_total, slope_h = head_item
            scores = head_scores(queries, keys_h, slope_h, distance, visible, score_scale)
            attn_probs = jnp.exp(scores - log_total[:, None])
            d_probs = contract_cols(grad_h, values_h)
            d_value = contract_rows(attn_probs.astype(jnp.bfloat16), grad_h)
            delta_sum = jnp.sum(d_probs * attn_probs, axis=-1, keepdims=True)
            d_scores = (attn_probs * (d_probs - delta_sum)).astype(jnp.bfloat16)
            d_query = jnp.dot(d_scores, keys_h, preferred_element_type=jnp.float32) * score_scale
            d_key = contract_rows(d_scores, queries) * score_scale
            return (d_query, d_key, d_value)

        d_query, d_key, d_value = lax.map(
            attend_back, (query_heads, key_heads, value_heads, d_attn_heads, log_totals, slopes)
        )
        key_rows, value_rows = (
            lax.psum_scatter(
                join_heads(d_key).astype(jnp.bfloat16), "seq", scatter_dimension=0, tiled=True
            ).astype(jnp.float32),
            lax.psum_scatter(
                join_heads(d_value).astype(jnp.bfloat16), "seq", scatter_dimension=0, tiled=True
            ).astype(jnp.float32),
        )
        query_low = join_heads(d_query).astype(jnp.bfloat16)
        value_low = value_rows.astype(jnp.bfloat16)
        d_qkv_low = jnp.concatenate([query_low, key_rows.astype(jnp.bfloat16), value_low], axis=1)
        g_qv_bias = jnp.stack(
            [
                jnp.sum(query_low.astype(jnp.float32), axis=0),
                jnp.sum(value_low.astype(jnp.float32), axis=0),
            ]
        ).reshape(2, heads_here, head_size)
        g_qkv = contract_rows(h_one_low, d_qkv_low).reshape(feat_width, 3, heads_here, head_size)
        d_h_one = lax.psum(contract_cols(d_qkv_low, back_qkv).astype(jnp.bfloat16), "mp").astype(
            jnp.float32
        )
        g_gain_one = jnp.sum(d_h_one * normed_one, axis=0)
        g_bias_one = jnp.sum(d_h_one, axis=0)
        input_rows.append(
            (d_resid + normalize_back(d_h_one, normed_one, inv_one, back_gain_one)).astype(
                jnp.bfloat16
            )
        )
        micro_grads = (
            g_gain_one,
            g_bias_one,
            g_qkv,
            g_qv_bias,
            g_out,
            g_out_bias,
            g_gain_two,
            g_bias_two,
            g_up,
            g_up_bias,
            g_down,
            g_down_bias,
        )
        if running is None:
            running = tuple(micro_grads)
        else:
            running = tuple(
                (total_arr + part_arr for total_arr, part_arr in zip(running, micro_grads))
            )
    running = (
        lax.psum_scatter(
            running[0].astype(jnp.bfloat16), ("dp", "seq"), scatter_dimension=0, tiled=True
        ).astype(jnp.float32),
        lax.psum_scatter(
            running[1].astype(jnp.bfloat16), ("dp", "seq"), scatter_dimension=0, tiled=True
        ).astype(jnp.float32),
        lax.psum_scatter(
            running[2].astype(jnp.bfloat16), ("dp", "seq"), scatter_dimension=0, tiled=True
        ).astype(jnp.float32),
        lax.psum_scatter(
            running[3].astype(jnp.bfloat16), ("dp", "seq"), scatter_dimension=2, tiled=True
        ).astype(jnp.float32),
        lax.psum_scatter(
            running[4].astype(jnp.bfloat16), ("dp", "seq"), scatter_dimension=2, tiled=True
        ).astype(jnp.float32),
        lax.psum_scatter(
            running[5].astype(jnp.bfloat16), ("dp", "seq"), scatter_dimension=0, tiled=True
        ).astype(jnp.float32),
        lax.psum_scatter(
            running[6].astype(jnp.bfloat16), ("dp", "seq"), scatter_dimension=0, tiled=True
        ).astype(jnp.float32),
        lax.psum_scatter(
            running[7].astype(jnp.bfloat16), ("dp", "seq"), scatter_dimension=0, tiled=True
        ).astype(jnp.float32),
        lax.psum_scatter(
            running[8].astype(jnp.bfloat16), ("dp", "seq"), scatter_dimension=0, tiled=True
        ).astype(jnp.float32),
        lax.psum_scatter(
            running[9].astype(jnp.bfloat16), ("dp", "seq"), scatter_dimension=1, tiled=True
        ).astype(jnp.float32),
        lax.psum_scatter(
            running[10].astype(jnp.bfloat16), ("dp", "seq"), scatter_dimension=1, tiled=True
        ).astype(jnp.float32),
        lax.psum_scatter(
            running[11].astype(jnp.bfloat16), ("dp", "seq"), scatter_dimension=0, tiled=True
        ).astype(jnp.float32),
    )
    output_rows = jnp.stack(outputs)[:, None]
    grad_rows = jnp.stack(input_rows)[:, None]
    return (
        output_rows,
        grad_rows,
        running[0],
        running[1],
        running[2],
        running[3],
        running[4],
        running[5],
        running[6],
        running[7],
        running[8],
        running[9],
        running[10],
        running[11],
    )


def solution(mesh):
    sizes = tuple(mesh.shape[axis] for axis in ("dp", "seq", "mp"))
    return jax.shard_map(
        local_fast if sizes == (4, 2, 4) else local,
        mesh=mesh,
        in_specs=(
            P(None, "dp", "seq", None),
            P(None, "dp"),
            P(None, "dp", "seq", None),
            P(("dp", "seq")),
            P(("dp", "seq")),
            P(("dp", "seq"), None, "mp", None),
            P(None, "mp", ("dp", "seq")),
            P("mp", None, ("dp", "seq")),
            P(("dp", "seq")),
            P(("dp", "seq")),
            P(("dp", "seq")),
            P(("dp", "seq"), "mp"),
            P("mp", ("dp", "seq")),
            P("mp", ("dp", "seq")),
            P(("dp", "seq")),
        ),
        out_specs=(
            P(None, "dp", "seq", None),
            P(None, "dp", "seq", None),
            P(("dp", "seq")),
            P(("dp", "seq")),
            P(("dp", "seq"), None, "mp", None),
            P(None, "mp", ("dp", "seq")),
            P("mp", None, ("dp", "seq")),
            P(("dp", "seq")),
            P(("dp", "seq")),
            P(("dp", "seq")),
            P(("dp", "seq"), "mp"),
            P("mp", ("dp", "seq")),
            P("mp", ("dp", "seq")),
            P(("dp", "seq")),
        ),
        check_vma=False,
    )
```

```python
import functools
import math

import jax
import jax.numpy as jnp
from jax import lax
from jax.experimental import pallas as pl
from jax.experimental.pallas import tpu as pltpu
from jax.sharding import PartitionSpec as P

eps_norm = 1e-05
masked_score = -1e30
inv_root_two = 0.7071067811865476
inv_root_tau = 0.3989422804014327


def contract_rows(left, right):
    return lax.dot_general(
        left, right, (((0,), (0,)), ((), ())), preferred_element_type=jnp.float32
    )


def contract_cols(left, right):
    return lax.dot_general(
        left, right, (((1,), (1,)), ((), ())), preferred_element_type=jnp.float32
    )


def normalize(values, gain_vec, shift_vec):
    row_mean = jnp.mean(values, axis=-1, keepdims=True)
    centered = values - row_mean
    variance = jnp.mean(centered * centered, axis=-1, keepdims=True)
    scale_inv = lax.rsqrt(variance + eps_norm)
    normed = centered * scale_inv
    return (normed * gain_vec + shift_vec, normed, scale_inv)


def normalize_back(grad_in, normed, scale_inv, gain_vec):
    scaled = grad_in * gain_vec
    return scale_inv * (
        scaled
        - jnp.mean(scaled, axis=-1, keepdims=True)
        - normed * jnp.mean(scaled * normed, axis=-1, keepdims=True)
    )


def gelu_slope(pre_act):
    cumulative = 0.5 * (1.0 + lax.erf(pre_act * inv_root_two))
    return cumulative + pre_act * jnp.exp(-0.5 * pre_act * pre_act) * inv_root_tau


def head_scores(queries, key_heads, slope_h, distance, visible, score_scale):
    raw_scores = contract_cols(queries, key_heads) * score_scale - slope_h * distance
    return jnp.where(visible, raw_scores, masked_score)


def split_heads(flat, count):
    return flat.reshape(flat.shape[0], count, -1).transpose(1, 0, 2)


def join_heads(stacked):
    return stacked.transpose(1, 0, 2).reshape(stacked.shape[1], -1)


log2e = math.log2(math.e)
hidden_distance = 1e30


def dot_nn(left, right):
    return lax.dot_general(
        left, right, (((1,), (0,)), ((), ())), preferred_element_type=jnp.float32
    )


def dot_nt(left, right):
    return lax.dot_general(
        left, right, (((1,), (1,)), ((), ())), preferred_element_type=jnp.float32
    )


times = {"merge": 4, "last_rows": 2}
special = {("restore", 1): 20, ("ring_add", 6): 10}
special.update({("pin", number): 40 for number in (3, 5, 7, 10, 12, 14, 17, 19, 21)})
special.update({("ring_add", number): 25 for number in (1, 3, 5)})
work_per_time = 1000000000
anywhere = pl.BlockSpec(memory_space=pl.ANY)


def fixed(step, *table):
    return (0, 0)


class Chain:
    last = None
    counts = {}


def call(
    kernel, name, grid, in_specs, out_specs, out_shape, values, table=None, scratch=(), **more
):
    earlier = [] if Chain.last is None else [Chain.last]
    number = Chain.counts.get(name, 0)
    Chain.counts[name] = number + 1
    time = special.get((name, number), times.get(name, 0))
    prefetched = 0 if table is None else 1
    first = len(in_specs) + prefetched
    count = len(earlier)

    def body(*refs):
        kernel(*refs[:first], *refs[first + count :])

    found = pl.pallas_call(
        body,
        grid_spec=pltpu.PrefetchScalarGridSpec(
            num_scalar_prefetch=prefetched,
            grid=grid,
            in_specs=list(in_specs) + [anywhere] * count,
            out_specs=out_specs,
            scratch_shapes=scratch,
        ),
        out_shape=out_shape,
        compiler_params=pltpu.CompilerParams(vmem_limit_bytes=50 << 20),
        cost_estimate=pl.CostEstimate(
            flops=int(time * work_per_time), bytes_accessed=0, transcendentals=0
        ),
        name=name,
        **more,
    )(*([] if table is None else [table]), *values, *earlier)
    Chain.last = found[0] if isinstance(found, (list, tuple)) else found
    return found


def array(shape, dtype=jnp.bfloat16):
    return jax.ShapeDtypeStruct(shape, dtype)


def dot_tn(left, right):
    return lax.dot_general(
        left, right, (((0,), (0,)), ((), ())), preferred_element_type=jnp.float32
    )


def error_function(values):
    bounded = jnp.clip(values, -3.832506856900711, 3.832506856900711)
    square = bounded * bounded
    above = jnp.full_like(square, 0.00022905065861350646)
    for factor in (
        0.0034082910107109506,
        0.050955695062380861,
        0.18520832239976145,
        1.128379143519084,
    ):
        above = above * square + factor
    below = jnp.full_like(square, -1.1791602954361697e-7)
    for factor in (
        0.000023547966471313185,
        0.0010179625278914885,
        0.014070470171167667,
        0.11098505178285362,
        0.49746925110067538,
        1.0,
    ):
        below = below * square + factor
    return bounded * above / below


def enter(values, gain_vec, bias_vec, core, half_rows):
    rows, width = values.shape

    def kernel(core_ref, values_ref, gain_ref, bias_ref, x_ref, h_ref):
        rows_low = values_ref[...]
        x_ref[...] = rows_low
        normed, _, _ = normalize(rows_low.astype(jnp.float32), gain_ref[...], bias_ref[...])
        h_ref[...] = normed.astype(h_ref.dtype)

    moved = pl.BlockSpec((half_rows, width), lambda step, core: (step ^ core[0], 0))
    whole = pl.BlockSpec((half_rows, width), lambda step, core: (step, 0))
    vector = pl.BlockSpec((1, width), fixed)
    return call(
        kernel,
        "enter",
        (rows // half_rows,),
        [moved, vector, vector],
        [whole, whole],
        [array((rows, width))] * 2,
        (values, gain_vec, bias_vec),
        core,
    )


def reorder(values, core, half_rows):
    rows, width = values.shape

    def kernel(core_ref, values_ref, out_ref):
        out_ref[...] = values_ref[...]

    return call(
        kernel,
        "reorder",
        (rows // half_rows,),
        [pl.BlockSpec((half_rows, width), lambda step, core: (step ^ core[0], 0))],
        pl.BlockSpec((half_rows, width), lambda step, core: (step, 0)),
        array((rows, width)),
        (values,),
        core,
    )


def restore(own, other, core, half_rows):
    micros, width = len(own), own[0].shape[1]

    def kernel(core_ref, *refs):
        out_ref = refs[-1]
        step = pl.program_id(0)
        mine = (step % 2) == core_ref[0]
        for micro in range(micros):
            here = step // 2 == micro

            @pl.when(here & mine)
            def _():
                out_ref[...] = refs[micro][...]

            @pl.when(here & jnp.logical_not(mine))
            def _():
                out_ref[...] = refs[micros + micro][...]

    piece = pl.BlockSpec((half_rows, width), fixed)
    return call(
        kernel,
        "restore",
        (2 * micros,),
        [pl.BlockSpec(memory_space=pltpu.SMEM)] + [piece] * (2 * micros),
        pl.BlockSpec((half_rows, width), lambda step: (step, 0)),
        array((2 * micros * half_rows, width)),
        (core, *own, *other),
    )


def pin(value):
    def kernel(*refs):
        pass

    return call(
        kernel,
        "pin",
        (1,),
        [anywhere],
        anywhere,
        array(value.shape, value.dtype),
        (value,),
        input_output_aliases={0: 0},
    )


def transpose_wide(values):
    rows, columns = values.shape

    def kernel(values_ref, out_ref):
        out_ref[...] = values_ref[...].T.astype(jnp.float32)

    return call(
        kernel,
        "transpose_wide",
        (4,),
        [pl.BlockSpec((rows, columns // 4), lambda step: (0, step))],
        pl.BlockSpec((columns // 4, rows), lambda step: (step, 0)),
        array((columns, rows), jnp.float32),
        (values,),
    )


def copy_wide(values, *earlier):
    rows, columns = values.shape

    def kernel(values_ref, *refs):
        refs[-1][...] = values_ref[...].astype(jnp.float32)

    piece = pl.BlockSpec((rows // 4, columns), lambda step: (step, 0))
    return call(
        kernel,
        "copy_wide",
        (4,),
        [piece] + [anywhere] * len(earlier),
        piece,
        array((rows, columns), jnp.float32),
        (values, *earlier),
    )


def widen(own, arrived, upper):
    rows, columns = own.shape

    def kernel(upper_ref, own_ref, arrived_ref, out_ref):
        @pl.when(upper_ref[0] == 0)
        def _():
            out_ref[:rows, :] = own_ref[...]
            out_ref[rows:, :] = arrived_ref[...]

        @pl.when(upper_ref[0] != 0)
        def _():
            out_ref[:rows, :] = arrived_ref[...]
            out_ref[rows:, :] = own_ref[...]

    piece = pl.BlockSpec((rows, columns), fixed)
    return call(
        kernel,
        "widen",
        (1,),
        [pl.BlockSpec(memory_space=pltpu.SMEM), piece, piece],
        pl.BlockSpec((2 * rows, columns), fixed),
        array((2 * rows, columns), own.dtype),
        (upper, own, arrived),
    )


def pack_sums(first_sums, norm_sums, hidden_sums, head_sums):
    width = hidden_sums.shape[1]
    inner = head_sums[0].shape[1] // 3

    def kernel(first0, first1, norm0, norm1, hidden_ref, heads0, heads1, out_ref):
        ones = first0[...] + first1[...]
        norms = norm0[...] + norm1[...]
        heads = heads0[...] + heads1[...]
        out_ref[0:2, :] = ones
        out_ref[2:3, :] = norms[2:3]
        out_ref[3:5, :] = norms[0:2]
        out_ref[5:6, :] = norms[3:4]
        out_ref[6:7, :] = hidden_ref[...]
        out_ref[7:8, :inner] = heads[:, :inner]
        out_ref[7:8, inner : 2 * inner] = heads[:, 2 * inner :]
        out_ref[7:8, 2 * inner :] = jnp.zeros((1, width - 2 * inner), jnp.float32)

    values = (*first_sums, *norm_sums, hidden_sums, *head_sums)
    return call(
        kernel,
        "pack_sums",
        (1,),
        [pl.BlockSpec(value.shape, fixed) for value in values],
        pl.BlockSpec((8, width), fixed),
        array((8, width), jnp.float32),
        values,
    )


def add_sums(own, arrived, rows):
    def kernel(own_ref, arrived_ref, out_ref):
        row = lax.broadcasted_iota(jnp.int32, own.shape, 0)
        out_ref[...] = own_ref[...] + jnp.where(row < rows, arrived_ref[...], 0.0)

    piece = pl.BlockSpec(own.shape, fixed)
    return call(
        kernel,
        "add_sums",
        (1,),
        [piece, piece],
        piece,
        array(own.shape, jnp.float32),
        (own, arrived),
    )


def far_halves(parts, table, item):
    rows, columns = parts.shape[0] // table.shape[0], parts.shape[1]
    half = pl.BlockSpec((rows // 2, columns), fixed)

    def kernel(table_ref, part_ref, top_ref, bottom_ref):
        top_ref[...] = part_ref[: rows // 2]
        bottom_ref[...] = part_ref[rows // 2 :]

    return call(
        kernel,
        "far_halves",
        (1,),
        [pl.BlockSpec((rows, columns), lambda step, table: (table[item], 0))],
        [half, half],
        [array((rows // 2, columns))] * 2,
        (parts,),
        table,
    )


def join(pieces, firsts):
    count = len(pieces)
    rows = sum(piece.shape[0] for piece in pieces)

    def kernel(firsts_ref, *refs):
        out_ref, sems = refs[count], refs[count + 1]
        copies = []
        for item in range(count):
            first = pl.multiple_of(firsts_ref[item], 128)
            target = out_ref.at[pl.ds(first, pieces[item].shape[0]), :]
            copies.append(pltpu.make_async_copy(refs[item], target, sems.at[item]))
        for copy in copies:
            copy.start()
        for copy in copies:
            copy.wait()

    return call(
        kernel,
        "join",
        (1,),
        [pl.BlockSpec(memory_space=pltpu.SMEM)] + [pl.BlockSpec(memory_space=pltpu.VMEM)] * count,
        anywhere,
        array((rows, pieces[0].shape[1])),
        (firsts, *pieces),
        scratch=[pltpu.SemaphoreType.DMA((count,))],
    )


def project(h_rows, weights, shift, inner):
    rows, width = h_rows.shape

    def kernel(h_ref, w_ref, shift_ref, q_ref, kv0_ref, kv1_ref):
        step = pl.program_id(0)
        low = (dot_nn(h_ref[...], w_ref[...]) + shift_ref[...]).astype(jnp.bfloat16)

        @pl.when(step == 0)
        def _():
            q_ref[...] = low

        @pl.when(step > 0)
        def _():
            kv0_ref[...] = low[: rows // 2]
            kv1_ref[...] = low[rows // 2 :]

    kv_spec = pl.BlockSpec((rows // 2, inner), lambda step: (0, jnp.maximum(step - 1, 0)))
    return call(
        kernel,
        "project",
        (3,),
        [
            pl.BlockSpec((rows, width), fixed),
            pl.BlockSpec((width, inner), lambda step: (0, step)),
            pl.BlockSpec((1, inner), lambda step: (0, step)),
        ],
        [pl.BlockSpec((rows, inner), fixed), kv_spec, kv_spec],
        [array((rows, inner)), array((rows // 2, 2 * inner)), array((rows // 2, 2 * inner))],
        (h_rows, weights, shift),
    )


def branch_shares(lefts, weights, columns, place, half_rows, tile, name):
    rows = sum(left.shape[0] for left in lefts)
    width = weights.shape[0]
    pairs = rows // (2 * half_rows)

    def kernel(*refs):
        left_refs, w_ref = refs[: len(lefts)], refs[len(lefts)]
        own_ref, other_ref = refs[-2:]
        at = 0
        for left_ref in left_refs:
            low = dot_nt(left_ref[...], w_ref[...]).astype(jnp.bfloat16)
            for half in range(left_ref.shape[0] // half_rows):
                pair, which = divmod(at, 2)
                target = own_ref if which == 0 else other_ref
                target[pair * half_rows : (pair + 1) * half_rows, :] = low[
                    half * half_rows : (half + 1) * half_rows
                ]
                at += 1

    out_spec = pl.BlockSpec((pairs * half_rows, tile), lambda step: (0, step))
    return call(
        kernel,
        name,
        (width // tile,),
        [pl.BlockSpec(left.shape, fixed) for left in lefts]
        + [pl.BlockSpec((tile, columns), lambda step: (step, place))],
        [out_spec, out_spec],
        [array((pairs * half_rows, width))] * 2,
        (*lefts, weights),
    )


def add_pair(own, arrived, micro, half_rows):
    width = own.shape[1]
    per_piece = arrived.shape[0] // half_rows
    rows = half_rows // 2

    def kernel(own_ref, arrived_ref, out_ref):
        total = own_ref[...].astype(jnp.float32) + arrived_ref[...].astype(jnp.float32)
        out_ref[...] = total.astype(out_ref.dtype)

    here = pl.BlockSpec((rows, width), lambda step: (2 * micro + step, 0))
    first = 2 * micro if per_piece > 1 else 0
    return call(
        kernel,
        "add_pair",
        (2,),
        [here, pl.BlockSpec((rows, width), lambda step: (first + step, 0))],
        pl.BlockSpec((rows, width), lambda step: (step, 0)),
        array((half_rows, width)),
        (own, arrived),
    )


def row_specs(half_rows, width, steps):
    rows = half_rows // steps
    here = pl.BlockSpec((rows, width), lambda step: (step, 0))
    vector = pl.BlockSpec((1, width), fixed)

    def at(micro):
        return pl.BlockSpec((rows, width), lambda step: (2 * micro * steps + step, 0))

    return here, vector, at


def second_norm(x_rows, pair, across, shift, gain_vec, bias_vec, micro, half_rows):
    width = x_rows.shape[1]
    here, vector, at = row_specs(half_rows, width, 4)

    def kernel(x_ref, pair_ref, across_ref, shift_ref, gain_ref, bias_ref, resid_ref, h_ref):
        branch = pair_ref[...].astype(jnp.float32) + across_ref[...].astype(jnp.float32)
        resid = x_ref[...].astype(jnp.float32) + (branch + shift_ref[...])
        resid_ref[...] = resid
        normed, _, _ = normalize(resid, gain_ref[...], bias_ref[...])
        h_ref[...] = normed.astype(h_ref.dtype)

    return call(
        kernel,
        "second_norm",
        (4,),
        [at(micro), here, here, vector, vector, vector],
        [here, here],
        [array((half_rows, width), jnp.float32), array((half_rows, width))],
        (x_rows, pair, across, shift, gain_vec, bias_vec),
    )


def expand(pieces, weights, shift, tile):
    rows = sum(piece.shape[0] for piece in pieces)
    width, hidden = weights.shape

    def kernel(*refs):
        piece_refs = refs[: len(pieces)]
        w_ref, shift_ref, act_ref, slope_ref, h_ref = refs[len(pieces) :]

        @pl.when(pl.program_id(0) == 0)
        def _():
            at = 0
            for piece in piece_refs:
                h_ref[at : at + piece.shape[0], :] = piece[...]
                at += piece.shape[0]

        up = dot_nn(h_ref[...], w_ref[...]) + shift_ref[...]
        cumulative = 0.5 * (1.0 + error_function(up * inv_root_two))
        act_ref[...] = (up * cumulative).astype(act_ref.dtype)
        density = jnp.exp(-0.5 * up * up) * inv_root_tau
        slope_ref[...] = (cumulative + up * density).astype(slope_ref.dtype)

    out_spec = pl.BlockSpec((rows, tile), lambda step: (0, step))
    return call(
        kernel,
        "expand",
        (hidden // tile,),
        [pl.BlockSpec(piece.shape, fixed) for piece in pieces]
        + [
            pl.BlockSpec((width, tile), lambda step: (0, step)),
            pl.BlockSpec((1, tile), lambda step: (0, step)),
        ],
        [out_spec, out_spec],
        [array((rows, hidden))] * 2,
        (*pieces, weights, shift),
        scratch=[pltpu.VMEM((rows, width), jnp.bfloat16)],
    )


def expand_back(grads, weights, slope, tile):
    rows, width = grads.shape
    hidden = weights.shape[1]

    def kernel(g_ref, w_ref, slope_ref, out_ref, sum_ref):
        low = (dot_nn(g_ref[...], w_ref[...]) * slope_ref[...].astype(jnp.float32)).astype(
            out_ref.dtype
        )
        out_ref[...] = low
        sum_ref[...] = jnp.sum(low.astype(jnp.float32), axis=0, keepdims=True)

    tile_spec = pl.BlockSpec((rows, tile), lambda step: (0, step))
    return call(
        kernel,
        "expand_back",
        (hidden // tile,),
        [
            pl.BlockSpec((rows, width), fixed),
            pl.BlockSpec((width, tile), lambda step: (0, step)),
            tile_spec,
        ],
        [tile_spec, pl.BlockSpec((1, tile), lambda step: (0, step))],
        [array((rows, hidden)), array((1, hidden), jnp.float32)],
        (grads, weights, slope),
    )


def weight_grad(lefts, rights, tile, name, whole=None, columns=None, place=0):
    width = lefts[0][0].shape[1]
    own_columns = rights[0][0].shape[1]
    columns = columns or own_columns

    def spec(piece, full):
        values, first, rows = piece
        if full:
            return pl.BlockSpec((rows, own_columns), lambda step: (first // rows, 0))
        return pl.BlockSpec((rows, tile), lambda step: (first // rows, step))

    def kernel(*refs):
        total = None
        for item in range(len(lefts)):
            part = dot_tn(refs[item][...], refs[len(lefts) + item][...])
            total = part if total is None else total + part
        refs[-1][...] = total.astype(refs[-1].dtype)

    values = [piece[0] for piece in (*lefts, *rights)]
    specs = [spec(piece, False) for piece in lefts] + [spec(piece, True) for piece in rights]
    more = {}
    if whole is not None:
        more["input_output_aliases"] = {len(values): 0}
        values.append(whole)
        specs.append(anywhere)
    return call(
        kernel,
        name,
        (width // tile,),
        specs,
        pl.BlockSpec((tile, own_columns), lambda step: (step, place)),
        array((width, columns)),
        values,
        **more,
    )


def second_norm_back(pair, across, resid, grads, gain_vec, micro, half_rows):
    width = resid.shape[1]
    here, vector, at = row_specs(half_rows, width, 4)

    def kernel(pair_ref, across_ref, resid_ref, g_ref, gain_ref, d_ref, low_ref, sum_ref):
        d_h = pair_ref[...].astype(jnp.float32) + across_ref[...].astype(jnp.float32)
        grad = g_ref[...].astype(jnp.float32)
        _, normed, scale_inv = normalize(resid_ref[...], gain_ref[...], 0.0)
        d_resid = grad + normalize_back(d_h, normed, scale_inv, gain_ref[...])
        low = d_resid.astype(low_ref.dtype)
        d_ref[...] = d_resid
        low_ref[...] = low

        @pl.when(pl.program_id(0) == 0)
        def _():
            sum_ref[...] = jnp.zeros_like(sum_ref)

        for item, value in enumerate((d_h * normed, d_h, low.astype(jnp.float32), grad)):
            sum_ref[item : item + 1, :] += jnp.sum(value, axis=0, keepdims=True)

    return call(
        kernel,
        "second_norm_back",
        (4,),
        [here, here, here, at(micro), vector],
        [here, here, pl.BlockSpec((4, width), fixed)],
        [
            array((half_rows, width), jnp.float32),
            array((half_rows, width)),
            array((4, width), jnp.float32),
        ],
        (pair, across, resid, grads, gain_vec),
    )


def attention_grad(pieces, weights, columns, place):
    rows = sum(piece.shape[0] for piece in pieces)
    width = weights.shape[0]

    def kernel(*refs):
        at = 0
        for piece in refs[: len(pieces)]:
            low = dot_nn(piece[...], refs[len(pieces)][...]).astype(jnp.bfloat16)
            refs[-1][at : at + piece.shape[0], :] = low
            at += piece.shape[0]

    return call(
        kernel,
        "attention_grad",
        (1,),
        [pl.BlockSpec(piece.shape, fixed) for piece in pieces]
        + [pl.BlockSpec((width, columns), lambda step: (0, place))],
        pl.BlockSpec((rows, columns), fixed),
        array((rows, columns)),
        (*pieces, weights),
    )


def merge(dq, dk, dv, more):
    rows, inner = dq.shape

    def kernel(dq_ref, dk_ref, dv_ref, more_ref, out_ref, sum_ref):
        low = out_ref.dtype
        parts = (
            dq_ref[...],
            (dk_ref[...] + more_ref[0].astype(jnp.float32)).astype(low),
            (dv_ref[...] + more_ref[1].astype(jnp.float32)).astype(low),
        )

        @pl.when(pl.program_id(0) == 0)
        def _():
            sum_ref[...] = jnp.zeros_like(sum_ref)

        for item, part in enumerate(parts):
            out_ref[:, item * inner : (item + 1) * inner] = part
            sum_ref[:, item * inner : (item + 1) * inner] += jnp.sum(
                part.astype(jnp.float32), axis=0, keepdims=True
            )

    piece = pl.BlockSpec((rows // 2, inner), lambda step: (step, 0))
    return call(
        kernel,
        "merge",
        (2,),
        [piece, piece, piece, pl.BlockSpec((2, rows // 2, inner), lambda step: (0, step, 0))],
        [
            pl.BlockSpec((rows // 2, 3 * inner), lambda step: (step, 0)),
            pl.BlockSpec((1, 3 * inner), fixed),
        ],
        [array((rows, 3 * inner)), array((1, 3 * inner), jnp.float32)],
        (dq, dk, dv, more),
    )


def first_norm_back(pair, across, x_rows, d_resid, gain_vec, micro, half_rows):
    width = x_rows.shape[1]
    here, vector, at = row_specs(half_rows, width, 4)

    def kernel(pair_ref, across_ref, x_ref, d_ref, gain_ref, out_ref, sum_ref):
        d_h = pair_ref[...].astype(jnp.float32) + across_ref[...].astype(jnp.float32)
        _, normed, scale_inv = normalize(x_ref[...].astype(jnp.float32), gain_ref[...], 0.0)
        total = d_ref[...] + normalize_back(d_h, normed, scale_inv, gain_ref[...])
        out_ref[...] = total.astype(out_ref.dtype)

        @pl.when(pl.program_id(0) == 0)
        def _():
            sum_ref[...] = jnp.zeros_like(sum_ref)

        for item, value in enumerate((d_h * normed, d_h)):
            sum_ref[item : item + 1, :] += jnp.sum(value, axis=0, keepdims=True)

    return call(
        kernel,
        "first_norm_back",
        (4,),
        [here, here, at(micro), here, vector],
        [here, pl.BlockSpec((2, width), fixed)],
        [array((half_rows, width)), array((2, width), jnp.float32)],
        (pair, across, x_rows, d_resid, gain_vec),
    )


def last_rows(resid, pair, across, shift):
    half_rows, width = resid.shape
    here, vector, _ = row_specs(half_rows, width, 4)

    def kernel(resid_ref, pair_ref, across_ref, shift_ref, out_ref):
        ffn = pair_ref[...].astype(jnp.float32) + across_ref[...].astype(jnp.float32)
        out_ref[...] = (resid_ref[...] + (ffn + shift_ref[...])).astype(out_ref.dtype)

    return call(
        kernel,
        "last_rows",
        (4,),
        [here, here, here, vector],
        here,
        array((half_rows, width)),
        (resid, pair, across, shift),
    )


def ring_add(parts, table, item, more, first=0, last=True):
    count = table.shape[0]
    rows, columns = parts.shape[0] // count, parts.shape[1]
    wide = jnp.float32

    def kernel(table_ref, part_ref, *refs):
        out_ref = refs[-1]
        total = part_ref[...].astype(wide)
        if more[0].shape[0] == rows:
            for value in refs[: len(more)]:
                total += value[...].astype(wide)
            out_ref[...] = total.astype(out_ref.dtype)
        else:
            out_ref[...] = total.astype(out_ref.dtype)
            half = more[0].shape[0]
            some = total[first : first + half] + refs[0][...].astype(wide)
            out_ref[first : first + half, :] = some.astype(out_ref.dtype)

    return call(
        kernel,
        "ring_add",
        (1,),
        [pl.BlockSpec((rows, columns), lambda step, table: (table[item], 0))]
        + [pl.BlockSpec(value.shape, fixed) for value in more],
        pl.BlockSpec((rows, columns), fixed),
        array((rows, columns), wide if last else jnp.bfloat16),
        (parts, *more),
        table,
    )


def fill_distance(place_ref, dist_ref, rows):
    own_first, other_first = place_ref[0], place_ref[1]
    prefix, flip = place_ref[2], place_ref[3]
    for block, first in enumerate((own_first, other_first)):
        shape = (rows, rows)
        key_pos = (lax.broadcasted_iota(jnp.int32, shape, 0) ^ flip) + first
        query_pos = (lax.broadcasted_iota(jnp.int32, shape, 1) ^ flip) + own_first
        visible = (key_pos <= query_pos) | (key_pos < prefix)
        gap = jnp.abs(query_pos - key_pos).astype(jnp.float32)
        dist_ref[block * rows : (block + 1) * rows, :] = jnp.where(visible, gap, hidden_distance)


def attend_kernel(place_ref, slope_ref, q_ref, k_ref, v_ref, ko_ref, vo_ref, out_ref, lse_ref, dist_ref, *, head_size):
    pair = pl.program_id(0)
    rows = q_ref.shape[0]

    @pl.when(pair == 0)
    def _():
        fill_distance(place_ref, dist_ref, rows)

    per_block = q_ref.shape[1] // head_size
    queries = q_ref[...]
    keys = jnp.concatenate([k_ref[...], ko_ref[...]], axis=0)
    values_t = jnp.concatenate([v_ref[...], vo_ref[...]], axis=0).T
    lane_head = lax.broadcasted_iota(jnp.int32, queries.shape, 1) // head_size
    parts = []
    for head in range(per_block):
        picked = jnp.where(lane_head == head, queries, jnp.zeros_like(queries))
        slope = slope_ref[pair * per_block + head]
        scores = dot_nt(keys, picked) * (log2e * head_size**-0.5) - dist_ref[...] * slope
        top = jnp.max(scores, axis=0, keepdims=True)
        weights = jnp.exp2(scores - top)
        total = jnp.sum(weights, axis=0, keepdims=True)
        head_out = dot_nn(values_t, weights.astype(jnp.bfloat16)) / total
        parts.append(head_out[head * head_size : (head + 1) * head_size])
        lse_ref[pl.ds(pair * per_block + head, 1), :] = top + jnp.log2(total)
    out_ref[...] = jnp.concatenate(parts, axis=0).T.astype(out_ref.dtype)


def attend_back_kernel(
    place_ref, slope_ref, q_ref, k_ref, v_ref, ko_ref, vo_ref, g_ref, lse_ref,
    dq_ref, dk_ref, dv_ref, other_ref, dist_ref, *, head_size
):
    pair = pl.program_id(0)
    rows = q_ref.shape[0]

    @pl.when(pair == 0)
    def _():
        fill_distance(place_ref, dist_ref, rows)

    per_block = q_ref.shape[1] // head_size
    queries, grads = q_ref[...], g_ref[...]
    keys = jnp.concatenate([k_ref[...], ko_ref[...]], axis=0)
    values = jnp.concatenate([v_ref[...], vo_ref[...]], axis=0)
    keys_t = keys.T
    lane_head = lax.broadcasted_iota(jnp.int32, queries.shape, 1) // head_size
    dq_parts = []
    d_keys, d_values = None, None
    for head in range(per_block):
        here = lane_head == head
        picked = jnp.where(here, queries, jnp.zeros_like(queries))
        picked_grad = jnp.where(here, grads, jnp.zeros_like(grads))
        slope = slope_ref[pair * per_block + head]
        scores = dot_nt(keys, picked) * (log2e * head_size**-0.5) - dist_ref[...] * slope
        probs = jnp.exp2(scores - lse_ref[pl.ds(pair * per_block + head, 1), :])
        weighted = dot_nt(values, picked_grad) * probs
        delta = jnp.sum(weighted, axis=0, keepdims=True)
        d_scores = (weighted - probs * delta).astype(jnp.bfloat16)
        value_part = dot_nn(probs.astype(jnp.bfloat16), picked_grad)
        key_part = dot_nn(d_scores, picked)
        d_values = value_part if d_values is None else d_values + value_part
        d_keys = key_part if d_keys is None else d_keys + key_part
        dq_part = dot_nn(keys_t, d_scores)
        dq_parts.append(dq_part[head * head_size : (head + 1) * head_size])
    scale = head_size**-0.5
    dq_ref[...] = (jnp.concatenate(dq_parts, axis=0).T * scale).astype(dq_ref.dtype)
    dk_ref[...] = (d_keys[:rows] * scale).astype(dk_ref.dtype)
    other_ref[0] = (d_keys[rows:] * scale).astype(other_ref.dtype)
    dv_ref[...] = d_values[:rows].astype(dv_ref.dtype)
    other_ref[1] = d_values[rows:].astype(other_ref.dtype)


def head_specs(queries, own_kv, head_size, micro):
    rows, inner = own_kv.shape[0], queries.shape[1]
    wide = 2 * head_size
    steps = inner // wide
    smem = pl.BlockSpec(memory_space=pltpu.SMEM)

    def at(first, row=0):
        return pl.BlockSpec((rows, wide), lambda step: (row, first + step))

    specs = [smem, smem, at(0, micro), at(0), at(steps), at(0), at(steps)]
    lse_spec = pl.BlockSpec((inner // head_size, rows), fixed)
    return rows, inner, steps, specs, at, lse_spec


def attend(queries, own_kv, other_kv, place, slopes, head_size, micro):
    rows, inner, steps, specs, at, lse_spec = head_specs(queries, own_kv, head_size, micro)
    return call(
        functools.partial(attend_kernel, head_size=head_size),
        "attend",
        (steps,),
        specs,
        [at(0), lse_spec],
        [array((rows, inner)), array((inner // head_size, rows), jnp.float32)],
        (place, slopes, queries, own_kv, own_kv, other_kv, other_kv),
        scratch=[pltpu.VMEM((2 * rows, rows), jnp.float32)],
    )


def attend_back(queries, own_kv, other_kv, grads, lse, place, slopes, head_size, micro):
    rows, inner, steps, specs, at, lse_spec = head_specs(queries, own_kv, head_size, micro)
    wide = 2 * head_size
    return call(
        functools.partial(attend_back_kernel, head_size=head_size),
        "attend_back",
        (steps,),
        specs + [at(0), lse_spec],
        [at(0), at(0), at(0), pl.BlockSpec((2, rows, wide), lambda step: (0, 0, step))],
        [
            array((rows, inner)),
            array((rows, inner), jnp.float32),
            array((rows, inner), jnp.float32),
            array((2, rows, inner)),
        ],
        (place, slopes, queries, own_kv, own_kv, other_kv, other_kv, grads, lse),
        scratch=[pltpu.VMEM((2 * rows, rows), jnp.float32)],
    )


def ring_places(dp_size, seq_size):
    places = []
    for seq in range(seq_size):
        line = range(dp_size) if seq % 2 == 0 else reversed(range(dp_size))
        places += [dp * seq_size + seq for dp in line]
    return places


def swap_pairs(size, step):
    return [(place, place ^ step) for place in range(size)]


class RingGather:
    def __init__(self, piece, table, ways):
        self.blocks, self.ways = table.shape[0], ways
        self.firsts = table * piece.shape[0]
        self.found, self.places = [piece], [self.firsts[0]]
        self.pair, self.hop = (piece, piece), 0

    def step(self):
        half = self.blocks // 2
        ahead, behind = self.pair
        middle = ahead.shape[0] // 2
        if self.hop > 0:
            ahead, behind = pin(ahead), pin(behind)
            self.found += [ahead, behind]
            self.places += [self.firsts[self.blocks - self.hop], self.firsts[self.hop]]
        self.hop += 1
        if self.hop == half:
            ahead, behind = ahead[:middle], behind[middle:]
            self.places += [self.firsts[half], self.firsts[half] + middle]
        self.pair = (
            lax.ppermute(ahead, ("dp", "seq"), self.ways[0]),
            lax.ppermute(behind, ("dp", "seq"), self.ways[1]),
        )

    def whole(self):
        return join([*self.found, *self.pair], jnp.stack(self.places).astype(jnp.int32))


class RingScatter:
    def __init__(self, parts, table, ways):
        self.parts, self.table, self.ways = parts, table, ways
        self.blocks = table.shape[0]
        self.rows = parts.shape[0] // self.blocks
        self.pair, self.hop = None, 0

    def step(self):
        half, middle = self.blocks // 2, self.rows // 2
        if self.hop == 0:
            ahead, behind = far_halves(self.parts, self.table, half)
        else:
            ahead, behind = (
                ring_add(self.parts, self.table, half + way * self.hop, [value], first, False)
                for way, value, first in ((-1, self.pair[0], 0), (1, self.pair[1], middle))
            )
        self.pair = (
            lax.ppermute(ahead, ("dp", "seq"), self.ways[0]),
            lax.ppermute(behind, ("dp", "seq"), self.ways[1]),
        )
        self.hop += 1

    def total(self):
        return ring_add(self.parts, self.table, 0, list(self.pair))


def local_fast(
    tokens,
    prefix,
    cotangent,
    ln1_gain,
    ln1_bias,
    qkv_weight,
    qv_bias,
    out_weight,
    out_bias,
    ln2_gain,
    ln2_bias,
    up_weight,
    up_bias,
    down_weight,
    down_bias,
):
    Chain.last, Chain.counts = None, {}
    low, wide = jnp.bfloat16, jnp.float32
    micros, _, tok_rows, width = tokens.shape
    heads, head_size = qv_bias.shape[1], qkv_weight.shape[3]
    inner = heads * head_size
    head_count = heads * lax.axis_size("mp")
    dp_size, seq_size = lax.axis_size("dp"), lax.axis_size("seq")
    blocks = dp_size * seq_size
    shard = width // blocks
    half_rows = tok_rows // 2
    all_rows = micros * tok_rows
    dp_at, seq_at, mp_at = lax.axis_index("dp"), lax.axis_index("seq"), lax.axis_index("mp")
    core_at = mp_at % 2
    core_swap, chip_swap = swap_pairs(4, 1), swap_pairs(4, 2)

    ring = ring_places(dp_size, seq_size)
    onward = [(ring[place], ring[(place + 1) % blocks]) for place in range(blocks)]
    backward = [(there, here) for here, there in onward]
    ways = (onward, backward)
    ring_at = jnp.where(seq_at == 0, dp_at, blocks - 1 - dp_at).astype(jnp.int32)
    along = (ring_at + jnp.arange(blocks, dtype=jnp.int32)) % blocks
    table = jnp.where(along < dp_size, along, blocks - 1 - along) * seq_size + along // dp_size
    table = table.astype(jnp.int32)
    core = core_at.astype(jnp.int32)[None]

    places = [
        jnp.stack(
            [
                seq_at * tok_rows,
                (1 - seq_at) * tok_rows,
                prefix[micro, 0],
                core_at * half_rows,
            ]
        ).astype(jnp.int32)
        for micro in range(micros)
    ]
    head_numbers = mp_at * heads + jnp.arange(heads, dtype=jnp.int32) + 1
    slopes = jnp.exp2(-8.0 * head_numbers.astype(wide) / head_count) * log2e

    def reduce_share(own, arrived, micro):
        pair = add_pair(own, arrived, micro, half_rows)
        return pair, lax.ppermute(pair, "mp", chip_swap)

    def scatter(parts):
        return lax.psum_scatter(parts, ("dp", "seq"), scatter_dimension=0, tiled=True)

    def swap_cores(values):
        return lax.ppermute(values, "mp", core_swap)

    small_parts = (ln1_gain, ln1_bias, out_bias, ln2_gain, ln2_bias, down_bias, qv_bias, up_bias)
    packed = jnp.concatenate([part.reshape(-1) for part in small_parts]).astype(wide)[None]
    packed = pin(packed)
    arrived = lax.ppermute(packed, "seq", swap_pairs(2, 1))
    attention_ring = RingGather(
        pin(
            jnp.concatenate(
                [qkv_weight.reshape(shard, 3 * inner), out_weight.reshape(inner, shard).T], axis=1
            )
        ),
        table,
        ways,
    )
    attention_ring.step()
    packed = widen(packed, arrived, seq_at.astype(jnp.int32)[None])
    arrived = lax.ppermute(packed, "dp", swap_pairs(4, 1))
    attention_ring.step()
    packed = widen(packed, arrived, (dp_at & 1).astype(jnp.int32)[None])
    arrived = lax.ppermute(packed, "dp", swap_pairs(4, 2))
    attention_ring.step()
    cot_rows = reorder(cotangent.reshape(all_rows, width), core, half_rows)
    packed = widen(packed, arrived, (dp_at >> 1).astype(jnp.int32)[None])
    attention_ring.step()
    gain_one, bias_one, bias_out, gain_two, bias_two, bias_down = [
        packed[:, item * shard : (item + 1) * shard].reshape(1, width) for item in range(6)
    ]
    first = 6 * shard
    qv_size = qv_bias.size
    qv_all = packed[:, first : first + qv_size].reshape((blocks,) + qv_bias.shape)
    qv_all = qv_all.transpose(1, 2, 0, 3).reshape(2, inner)
    up_all = packed[:, first + qv_size :].reshape((blocks,) + up_bias.shape)
    up_shift = up_all.transpose(1, 0, 2).reshape(1, -1)
    qkv_shift = jnp.concatenate([qv_all[0], jnp.zeros((inner,), wide), qv_all[1]])[None]
    x_rows, h_one = enter(tokens.reshape(all_rows, width), gain_one, bias_one, core, half_rows)
    attention_full = attention_ring.whole()
    queries, *own_kv = project(h_one, attention_full, qkv_shift, inner)
    other_kv = [lax.ppermute(value, "seq", [(0, 1)]) for value in own_kv]

    attn, lse = [], []
    for micro in range(micros):
        attn_here, lse_here = attend(
            queries, own_kv[micro], other_kv[micro], places[micro], slopes, head_size, micro
        )
        attn.append(attn_here)
        lse.append(lse_here)
        if micro == 0:
            up_ring = RingGather(pin(up_weight), table, ways)
            up_ring.step()
    own, other = branch_shares(attn, attention_full, inner, 3, half_rows, 512, "out_shares")
    arrived = swap_cores(other)
    up_ring.step()
    shares = [reduce_share(own, arrived, micro) for micro in range(micros)]
    resid, h_two = [], []
    for micro in range(micros):
        resid_here, h_here = second_norm(
            x_rows, *shares[micro], bias_out, gain_two, bias_two, micro, half_rows
        )
        resid.append(resid_here)
        h_two += [h_here, swap_cores(h_here)]
        up_ring.step()
    up_full = up_ring.whole()
    down_ring = RingGather(pin(down_weight.T), table, ways)
    down_ring.step()
    act, slope = expand(h_two, up_full, up_shift, 256)
    down_ring.step()
    down_parts = weight_grad([(cot_rows, 0, all_rows)], [(act, 0, all_rows)], 256, "down_grad")
    down_ring.step()
    down_ring.step()
    down_t = down_ring.whole()
    g_down_t = scatter(pin(down_parts))
    d_up, sum_up = expand_back(cot_rows, down_t, slope, 256)
    own, other = branch_shares([d_up], up_full, d_up.shape[1], 0, half_rows, 256, "up_shares")
    arrived = swap_cores(other)
    shares = [reduce_share(own, arrived, micro) for micro in range(micros)]
    ffn_own, other = branch_shares([act], down_t, act.shape[1], 0, half_rows, 256, "down_shares")
    ffn_arrived = swap_cores(other)

    norm_sums, d_resid, d_branch, backs = [], [], [], []
    d_qkv, sum_qkv, output_rows = [], [], []
    for micro in range(micros):
        if micro == 1:
            up_parts = weight_grad(
                [(piece, 0, half_rows) for piece in h_two],
                [(d_up, item * half_rows, half_rows) for item in range(2 * micros)],
                256,
                "up_grad",
            )
            g_up = scatter(up_parts)
        d_here, d_low, sums = second_norm_back(
            *shares[micro], resid[micro], cot_rows, gain_two, micro, half_rows
        )
        norm_sums.append(sums)
        d_resid.append(d_here)
        d_branch += [d_low, swap_cores(d_low)]
        d_attn = attention_grad(d_branch[-2:], attention_full, inner, 3)
        if micro == 1:
            ffn_shares = [reduce_share(ffn_own, ffn_arrived, item) for item in range(micros)]
        dq, dk, dv, more = attend_back(
            queries,
            own_kv[micro],
            other_kv[micro],
            d_attn,
            lse[micro],
            places[micro],
            slopes,
            head_size,
            micro,
        )
        backs.append((dq, dk, dv, lax.ppermute(more, "seq", [(1, 0)])))
    d_here, sums = merge(*backs[0])
    d_qkv.append(d_here)
    sum_qkv.append(sums)
    ring_columns = attention_full.shape[1]
    out_parts = weight_grad(
        [(piece, 0, half_rows) for piece in d_branch],
        [(value, half * half_rows, half_rows) for value in attn for half in range(2)],
        512,
        "out_grad",
        columns=ring_columns,
        place=3,
    )
    for micro in range(micros):
        output_rows.append(last_rows(resid[micro], *ffn_shares[micro], bias_down))
    output_other = [swap_cores(piece) for piece in output_rows]
    d_here, sums = merge(*backs[1])
    d_qkv.append(d_here)
    sum_qkv.append(sums)
    attention_parts = weight_grad(
        [(h_one, micro * tok_rows, tok_rows) for micro in range(micros)],
        [(value, 0, tok_rows) for value in d_qkv],
        256,
        "qkv_grad",
        whole=out_parts,
        columns=ring_columns,
    )
    attention_grads = RingScatter(attention_parts, table, ways)
    attention_grads.step()
    own, other = branch_shares(
        d_qkv, attention_full, 3 * inner, 0, half_rows, 256, "qkv_shares"
    )
    arrived = swap_cores(other)
    attention_grads.step()
    shares = [reduce_share(own, arrived, micro) for micro in range(micros)]
    g_down_wide = transpose_wide(g_down_t)
    attention_grads.step()
    output = restore(output_rows, output_other, core, half_rows)
    first_sums, input_rows = [], []
    for micro in range(micros):
        rows_here, sums = first_norm_back(
            *shares[micro], x_rows, d_resid[micro], gain_one, micro, half_rows
        )
        first_sums.append(sums)
        input_rows.append(rows_here)
    input_other = [swap_cores(piece) for piece in input_rows]
    small = pack_sums(first_sums, norm_sums, sum_up, sum_qkv)
    arrived = swap_cores(small)
    attention_grads.step()
    small = add_sums(small, arrived, 6)
    arrived = lax.ppermute(small, "seq", swap_pairs(2, 1))
    input_grad = restore(input_rows, input_other, core, half_rows)
    small = add_sums(small, arrived, 8)
    arrived = lax.ppermute(small, "dp", swap_pairs(4, 1))
    g_attention = attention_grads.total()
    small = add_sums(small, arrived, 8)
    arrived = lax.ppermute(small, "dp", swap_pairs(4, 2))
    small = add_sums(small, arrived, 8)
    block = dp_at * seq_size + seq_at

    def own_part(values, axis):
        extent = values.shape[axis] // blocks
        return lax.dynamic_slice_in_dim(values, block * extent, extent, axis=axis)

    vector_grads = own_part(small[:6], 1)
    up_bias_grad = own_part(small[6].reshape(-1, blocks * up_bias.shape[1]), 1)
    qv_grad = own_part(small[7, : 2 * inner].reshape(2, heads, head_size), 2)
    finished = (
        vector_grads[0],
        vector_grads[1],
        g_attention[:, : 3 * inner].reshape(qkv_weight.shape),
        qv_grad,
        g_attention[:, 3 * inner :].T.reshape(out_weight.shape),
        vector_grads[2],
        vector_grads[3],
        vector_grads[4],
        up_bias_grad,
        vector_grads[5],
    )
    g_up_wide = copy_wide(g_up, finished[2], finished[4])
    return (
        output.reshape(tokens.shape),
        input_grad.reshape(tokens.shape),
        *finished[:8],
        g_up_wide,
        finished[8],
        g_down_wide,
        finished[9],
    )


def local(
    tokens,
    prefix,
    cotangent,
    ln1_gain,
    ln1_bias,
    qkv_weight,
    qv_bias,
    out_weight,
    out_bias,
    ln2_gain,
    ln2_bias,
    up_weight,
    up_bias,
    down_weight,
    down_bias,
):
    gathered = (
        lax.all_gather(ln1_gain, ("dp", "seq"), axis=0, tiled=True),
        lax.all_gather(ln1_bias, ("dp", "seq"), axis=0, tiled=True),
        lax.all_gather(qkv_weight, ("dp", "seq"), axis=0, tiled=True),
        lax.all_gather(qv_bias, ("dp", "seq"), axis=2, tiled=True),
        lax.all_gather(out_weight, ("dp", "seq"), axis=2, tiled=True),
        lax.all_gather(out_bias, ("dp", "seq"), axis=0, tiled=True),
        lax.all_gather(ln2_gain, ("dp", "seq"), axis=0, tiled=True),
        lax.all_gather(ln2_bias, ("dp", "seq"), axis=0, tiled=True),
        lax.all_gather(up_weight, ("dp", "seq"), axis=0, tiled=True),
        lax.all_gather(up_bias, ("dp", "seq"), axis=1, tiled=True),
        lax.all_gather(down_weight, ("dp", "seq"), axis=1, tiled=True),
        lax.all_gather(down_bias, ("dp", "seq"), axis=0, tiled=True),
    )
    tok_rows = tokens.shape[2]
    feat_width = tokens.shape[3]
    seq_length = tok_rows * lax.axis_size("seq")
    heads_here = qv_bias.shape[1]
    head_size = qkv_weight.shape[3]
    head_count = heads_here * lax.axis_size("mp")
    inner = heads_here * head_size
    score_scale = head_size ** (-0.5)
    first_head = lax.axis_index("mp") * heads_here
    slopes = jnp.exp2(
        -8.0
        * (first_head + jnp.arange(heads_here, dtype=jnp.int32) + 1).astype(jnp.float32)
        / head_count
    )
    own_start = lax.axis_index("seq") * tok_rows
    query_pos = own_start + jnp.arange(tok_rows, dtype=jnp.int32)
    key_pos = jnp.arange(seq_length, dtype=jnp.int32)
    distance = jnp.abs(query_pos[:, None] - key_pos[None, :]).astype(jnp.float32)
    causal = key_pos[None, :] <= query_pos[:, None]
    gain_one = gathered[0].astype(jnp.float32)
    bias_one = gathered[1].astype(jnp.float32)
    qkv_flat = gathered[2].reshape(feat_width, 3 * inner)
    bias_qv = gathered[3].astype(jnp.float32).reshape(2, inner)
    qkv_shift = jnp.concatenate([bias_qv[0], jnp.zeros((inner,), jnp.float32), bias_qv[1]])
    out_flat = gathered[4].reshape(inner, feat_width)
    bias_out = gathered[5].astype(jnp.float32)
    gain_two = gathered[6].astype(jnp.float32)
    bias_two = gathered[7].astype(jnp.float32)
    up_mat = gathered[8]
    up_shift = gathered[9].astype(jnp.float32).reshape(-1)
    down_mat = gathered[10]
    bias_down = gathered[11].astype(jnp.float32)
    saved = []
    outputs = []
    for micro_idx in range(tokens.shape[0]):
        x_rows = tokens[micro_idx, 0].astype(jnp.float32)
        h_one, normed_one, inv_one = normalize(x_rows, gain_one, bias_one)
        h_one_low = h_one.astype(jnp.bfloat16)
        qkv_low = (
            jnp.dot(h_one_low, qkv_flat, preferred_element_type=jnp.float32) + qkv_shift
        ).astype(jnp.bfloat16)
        key_all, value_all = (
            lax.all_gather(qkv_low[:, inner : 2 * inner], "seq", axis=0, tiled=True),
            lax.all_gather(qkv_low[:, 2 * inner :], "seq", axis=0, tiled=True),
        )
        query_heads = split_heads(qkv_low[:, :inner], heads_here)
        key_heads = split_heads(key_all, heads_here)
        value_heads = split_heads(value_all, heads_here)
        visible = causal | (key_pos[None, :] < prefix[micro_idx, 0])

        def attend(head_item):
            queries, keys_h, values_h, slope_h = head_item
            scores = head_scores(queries, keys_h, slope_h, distance, visible, score_scale)
            row_max = jnp.max(scores, axis=-1, keepdims=True)
            exp_scores = jnp.exp(scores - row_max)
            row_total = jnp.sum(exp_scores, axis=-1, keepdims=True)
            attn_probs = exp_scores / row_total
            head_out = jnp.dot(
                attn_probs.astype(jnp.bfloat16), values_h, preferred_element_type=jnp.float32
            )
            return (head_out.astype(jnp.bfloat16), (row_max + jnp.log(row_total))[:, 0])

        head_outs, log_totals = lax.map(attend, (query_heads, key_heads, value_heads, slopes))
        attn_low = join_heads(head_outs)
        branch = (
            lax.psum(
                jnp.dot(attn_low, out_flat, preferred_element_type=jnp.float32).astype(
                    jnp.bfloat16
                ),
                "mp",
            ).astype(jnp.float32)
            + bias_out
        )
        resid = x_rows + branch
        h_two, normed_two, inv_two = normalize(resid, gain_two, bias_two)
        h_two_low = h_two.astype(jnp.bfloat16)
        up_pre = jnp.dot(h_two_low, up_mat, preferred_element_type=jnp.float32) + up_shift
        act_low = jax.nn.gelu(up_pre, approximate=False).astype(jnp.bfloat16)
        ffn_out = (
            lax.psum(
                jnp.dot(act_low, down_mat, preferred_element_type=jnp.float32).astype(jnp.bfloat16),
                "mp",
            ).astype(jnp.float32)
            + bias_down
        )
        outputs.append((resid + ffn_out).astype(jnp.bfloat16))
        saved.append(
            (
                normed_one,
                inv_one,
                h_one_low,
                query_heads,
                key_heads,
                value_heads,
                visible,
                log_totals,
                attn_low,
                normed_two,
                inv_two,
                h_two_low,
                up_pre,
                act_low,
            )
        )
    regathered = (
        lax.all_gather(ln1_gain, ("dp", "seq"), axis=0, tiled=True),
        lax.all_gather(ln1_bias, ("dp", "seq"), axis=0, tiled=True),
        lax.all_gather(qkv_weight, ("dp", "seq"), axis=0, tiled=True),
        lax.all_gather(qv_bias, ("dp", "seq"), axis=2, tiled=True),
        lax.all_gather(out_weight, ("dp", "seq"), axis=2, tiled=True),
        lax.all_gather(out_bias, ("dp", "seq"), axis=0, tiled=True),
        lax.all_gather(ln2_gain, ("dp", "seq"), axis=0, tiled=True),
        lax.all_gather(ln2_bias, ("dp", "seq"), axis=0, tiled=True),
        lax.all_gather(up_weight, ("dp", "seq"), axis=0, tiled=True),
        lax.all_gather(up_bias, ("dp", "seq"), axis=1, tiled=True),
        lax.all_gather(down_weight, ("dp", "seq"), axis=1, tiled=True),
        lax.all_gather(down_bias, ("dp", "seq"), axis=0, tiled=True),
    )
    back_gain_one = regathered[0].astype(jnp.float32)
    back_qkv = regathered[2].reshape(feat_width, 3 * inner)
    back_out = regathered[4].reshape(inner, feat_width)
    back_gain_two = regathered[6].astype(jnp.float32)
    back_up = regathered[8]
    back_down = regathered[10]
    up_bias_shape = regathered[9].shape
    running = None
    input_rows = []
    for micro_idx in range(tokens.shape[0]):
        (
            normed_one,
            inv_one,
            h_one_low,
            query_heads,
            key_heads,
            value_heads,
            visible,
            log_totals,
            attn_low,
            normed_two,
            inv_two,
            h_two_low,
            up_pre,
            act_low,
        ) = saved[micro_idx]
        grad_out = cotangent[micro_idx, 0]
        grad_full = grad_out.astype(jnp.float32)
        g_down_bias = jnp.sum(grad_full, axis=0)
        g_down = contract_rows(act_low, grad_out)
        d_up_low = (contract_cols(grad_out, back_down) * gelu_slope(up_pre)).astype(jnp.bfloat16)
        g_up_bias = jnp.sum(d_up_low.astype(jnp.float32), axis=0).reshape(up_bias_shape)
        g_up = contract_rows(h_two_low, d_up_low)
        d_h_two = lax.psum(contract_cols(d_up_low, back_up).astype(jnp.bfloat16), "mp").astype(
            jnp.float32
        )
        g_gain_two = jnp.sum(d_h_two * normed_two, axis=0)
        g_bias_two = jnp.sum(d_h_two, axis=0)
        d_resid = grad_full + normalize_back(d_h_two, normed_two, inv_two, back_gain_two)
        d_branch_low = d_resid.astype(jnp.bfloat16)
        g_out_bias = jnp.sum(d_branch_low.astype(jnp.float32), axis=0)
        g_out = contract_rows(attn_low, d_branch_low).reshape(heads_here, head_size, feat_width)
        d_attn_heads = split_heads(
            contract_cols(d_branch_low, back_out).astype(jnp.bfloat16), heads_here
        )

        def attend_back(head_item):
            queries, keys_h, values_h, grad_h, log_total, slope_h = head_item
            scores = head_scores(queries, keys_h, slope_h, distance, visible, score_scale)
            attn_probs = jnp.exp(scores - log_total[:, None])
            d_probs = contract_cols(grad_h, values_h)
            d_value = contract_rows(attn_probs.astype(jnp.bfloat16), grad_h)
            delta_sum = jnp.sum(d_probs * attn_probs, axis=-1, keepdims=True)
            d_scores = (attn_probs * (d_probs - delta_sum)).astype(jnp.bfloat16)
            d_query = jnp.dot(d_scores, keys_h, preferred_element_type=jnp.float32) * score_scale
            d_key = contract_rows(d_scores, queries) * score_scale
            return (d_query, d_key, d_value)

        d_query, d_key, d_value = lax.map(
            attend_back, (query_heads, key_heads, value_heads, d_attn_heads, log_totals, slopes)
        )
        key_rows, value_rows = (
            lax.psum_scatter(
                join_heads(d_key).astype(jnp.bfloat16), "seq", scatter_dimension=0, tiled=True
            ).astype(jnp.float32),
            lax.psum_scatter(
                join_heads(d_value).astype(jnp.bfloat16), "seq", scatter_dimension=0, tiled=True
            ).astype(jnp.float32),
        )
        query_low = join_heads(d_query).astype(jnp.bfloat16)
        value_low = value_rows.astype(jnp.bfloat16)
        d_qkv_low = jnp.concatenate([query_low, key_rows.astype(jnp.bfloat16), value_low], axis=1)
        g_qv_bias = jnp.stack(
            [
                jnp.sum(query_low.astype(jnp.float32), axis=0),
                jnp.sum(value_low.astype(jnp.float32), axis=0),
            ]
        ).reshape(2, heads_here, head_size)
        g_qkv = contract_rows(h_one_low, d_qkv_low).reshape(feat_width, 3, heads_here, head_size)
        d_h_one = lax.psum(contract_cols(d_qkv_low, back_qkv).astype(jnp.bfloat16), "mp").astype(
            jnp.float32
        )
        g_gain_one = jnp.sum(d_h_one * normed_one, axis=0)
        g_bias_one = jnp.sum(d_h_one, axis=0)
        input_rows.append(
            (d_resid + normalize_back(d_h_one, normed_one, inv_one, back_gain_one)).astype(
                jnp.bfloat16
            )
        )
        micro_grads = (
            g_gain_one,
            g_bias_one,
            g_qkv,
            g_qv_bias,
            g_out,
            g_out_bias,
            g_gain_two,
            g_bias_two,
            g_up,
            g_up_bias,
            g_down,
            g_down_bias,
        )
        if running is None:
            running = tuple(micro_grads)
        else:
            running = tuple(
                (total_arr + part_arr for total_arr, part_arr in zip(running, micro_grads))
            )
    running = (
        lax.psum_scatter(
            running[0].astype(jnp.bfloat16), ("dp", "seq"), scatter_dimension=0, tiled=True
        ).astype(jnp.float32),
        lax.psum_scatter(
            running[1].astype(jnp.bfloat16), ("dp", "seq"), scatter_dimension=0, tiled=True
        ).astype(jnp.float32),
        lax.psum_scatter(
            running[2].astype(jnp.bfloat16), ("dp", "seq"), scatter_dimension=0, tiled=True
        ).astype(jnp.float32),
        lax.psum_scatter(
            running[3].astype(jnp.bfloat16), ("dp", "seq"), scatter_dimension=2, tiled=True
        ).astype(jnp.float32),
        lax.psum_scatter(
            running[4].astype(jnp.bfloat16), ("dp", "seq"), scatter_dimension=2, tiled=True
        ).astype(jnp.float32),
        lax.psum_scatter(
            running[5].astype(jnp.bfloat16), ("dp", "seq"), scatter_dimension=0, tiled=True
        ).astype(jnp.float32),
        lax.psum_scatter(
            running[6].astype(jnp.bfloat16), ("dp", "seq"), scatter_dimension=0, tiled=True
        ).astype(jnp.float32),
        lax.psum_scatter(
            running[7].astype(jnp.bfloat16), ("dp", "seq"), scatter_dimension=0, tiled=True
        ).astype(jnp.float32),
        lax.psum_scatter(
            running[8].astype(jnp.bfloat16), ("dp", "seq"), scatter_dimension=0, tiled=True
        ).astype(jnp.float32),
        lax.psum_scatter(
            running[9].astype(jnp.bfloat16), ("dp", "seq"), scatter_dimension=1, tiled=True
        ).astype(jnp.float32),
        lax.psum_scatter(
            running[10].astype(jnp.bfloat16), ("dp", "seq"), scatter_dimension=1, tiled=True
        ).astype(jnp.float32),
        lax.psum_scatter(
            running[11].astype(jnp.bfloat16), ("dp", "seq"), scatter_dimension=0, tiled=True
        ).astype(jnp.float32),
    )
    output_rows = jnp.stack(outputs)[:, None]
    grad_rows = jnp.stack(input_rows)[:, None]
    return (
        output_rows,
        grad_rows,
        running[0],
        running[1],
        running[2],
        running[3],
        running[4],
        running[5],
        running[6],
        running[7],
        running[8],
        running[9],
        running[10],
        running[11],
    )


def solution(mesh):
    sizes = tuple(mesh.shape[axis] for axis in ("dp", "seq", "mp"))
    return jax.shard_map(
        local_fast if sizes == (4, 2, 4) else local,
        mesh=mesh,
        in_specs=(
            P(None, "dp", "seq", None),
            P(None, "dp"),
            P(None, "dp", "seq", None),
            P(("dp", "seq")),
            P(("dp", "seq")),
            P(("dp", "seq"), None, "mp", None),
            P(None, "mp", ("dp", "seq")),
            P("mp", None, ("dp", "seq")),
            P(("dp", "seq")),
            P(("dp", "seq")),
            P(("dp", "seq")),
            P(("dp", "seq"), "mp"),
            P("mp", ("dp", "seq")),
            P("mp", ("dp", "seq")),
            P(("dp", "seq")),
        ),
        out_specs=(
            P(None, "dp", "seq", None),
            P(None, "dp", "seq", None),
            P(("dp", "seq")),
            P(("dp", "seq")),
            P(("dp", "seq"), None, "mp", None),
            P(None, "mp", ("dp", "seq")),
            P("mp", None, ("dp", "seq")),
            P(("dp", "seq")),
            P(("dp", "seq")),
            P(("dp", "seq")),
            P(("dp", "seq"), "mp"),
            P("mp", ("dp", "seq")),
            P("mp", ("dp", "seq")),
            P(("dp", "seq")),
        ),
        check_vma=False,
    )
```
